32 devices in a mesh: blk: 4 (over y, x), uly: 8 (over z, core).
Axes of the slice: x: 2, y: 2, z: 4, core: 2. Of those that a mesh axis runs over, the one named last changes fastest.
Arguments:
- query_proj: bfloat16 [2048, 1024], P(('blk', 'uly')), may hold values from -8 to 8
- key_proj: bfloat16 [2048, 1024], P(('blk', 'uly')), may hold values from -8 to 8
- value_proj: bfloat16 [2048, 1024], P(('blk', 'uly')), may hold values from -6 to 6
- attn_output: bfloat16 [2048, 1024], P(('blk', 'uly')), may hold values from -6 to 6
- out_grad: bfloat16 [2048, 1024], P(('blk', 'uly')), may hold values from -6 to 6
- random_blocks: int32 [16, 3], replicated, may hold values from 0 to 14, as said below
Outputs:
- query_grad: bfloat16 [2048, 1024], P(('blk', 'uly'))
- key_grad: bfloat16 [2048, 1024], P(('blk', 'uly'))
- value_grad: bfloat16 [2048, 1024], P(('blk', 'uly'))
The draws below stay inside these ranges and needn't reach their ends.
Inputs may be any that keep to these rules, and one draw needn't show every extreme that they name: `random_blocks`: every entry of row i names a block below i; row 0 names only block 0. The rows of one shard of blk (4 rows in a row, aligned) name at most 2 distinct blocks that lie in any one other shard, exactly 2 that lie in the shard just before theirs, and the rows of the last shard name exactly 2 that lie in the first shard.
All inputs are finite; a program needn't handle non-finite values.
Results may differ from the reference program's by a relative error of at most 0.005.
Values may be sent and summed in bfloat16 or wider, within the bound.
A program may use at most 64 MiB of HBM per device.

```python
import jax
import jax.numpy as jnp
from jax import lax

HD = 128
HEADS = 8
D = 1024
BLOCK = 128
RAND = 3
CAP = 2
SHARD = 512
SEQ = 2048
NB = 16


def pair_fields(key):
    base = jax.random.fold_in(key, 1234)
    draw_one, draw_two = jax.random.split(base, 2)
    full_width = HEADS * HD
    queries = jnp.clip(jax.random.normal(draw_one, (SEQ, full_width), jnp.float32), -4.0, 4.0)
    keys_drawn = jnp.clip(jax.random.normal(draw_two, (SEQ, full_width), jnp.float32), -4.0, 4.0)
    return (queries, keys_drawn)


def draw_query_proj(key, part):
    return pair_fields(key)[0].astype(jnp.bfloat16)


def draw_key_proj(key, part):
    return pair_fields(key)[1].astype(jnp.bfloat16)


def draw_random_blocks(key, part):
    per_shard = SHARD // BLOCK
    shard_count = NB // per_shard
    keys_all = jax.random.split(jax.random.fold_in(key, 77), 5)
    offsets = jax.random.randint(keys_all[0], (shard_count, shard_count), 0, per_shard, dtype=jnp.int32)
    block_ids = jnp.arange(NB, dtype=jnp.int32)
    shard_of = block_ids // per_shard
    local_of = block_ids % per_shard
    coin = jax.random.randint(keys_all[1], (NB, RAND), 0, 2, dtype=jnp.int32)
    source = jax.random.randint(keys_all[2], (NB, RAND), 0, jnp.maximum(shard_of, 1)[:, None], dtype=jnp.int32)
    slot = jax.random.randint(keys_all[3], (NB, RAND), 0, CAP, dtype=jnp.int32)
    local_pick = jax.random.randint(keys_all[4], (NB, RAND), 0, jnp.maximum(local_of, 1)[:, None], dtype=jnp.int32) + (shard_of * per_shard)[:, None]
    pool_offset = offsets[shard_of[:, None], source]
    remote_block = source * per_shard + (pool_offset + slot) % per_shard
    use_remote = (shard_of[:, None] >= 1) & ((local_of[:, None] == 0) | (coin == 1))
    entries = jnp.where(use_remote, remote_block, jnp.where(local_of[:, None] >= 1, local_pick, 0))
    previous = jnp.maximum(shard_of - 1, 0)
    forced = previous * per_shard + (offsets[shard_of, previous] + local_of) % per_shard
    force_here = (shard_of >= 1) & (local_of < CAP)
    entries = entries.at[:, 0].set(jnp.where(force_here, forced, entries[:, 0]))
    first_forced = (offsets[shard_of, 0] + local_of) % per_shard
    force_first = (shard_of == shard_count - 1) & (local_of < CAP)
    entries = entries.at[:, 1].set(jnp.where(force_first, first_forced, entries[:, 1]))
    entries = entries.at[NB - 1, RAND - 1].set(NB - 2)
    return entries.astype(jnp.int32)


def steps_of(key, shape, shards, smallest, top_value):
    def one(axis_at, parts):
        heights = jax.random.uniform(jax.random.fold_in(jax.random.fold_in(key, 6), axis_at), (parts,), jnp.float32, smallest / len(shards), top_value / len(shards))
        return jnp.repeat(jnp.exp(heights), shape[axis_at] // parts).reshape((-1,) + (1,) * (len(shape) - axis_at - 1))

    level = one(*shards[0])
    for cut in shards[1:]:
        level = level * one(*cut)
    return level


def noise(own_key, dims, width, limit, pieces=(), held_as=jnp.bfloat16):
    level = steps_of(own_key, dims, pieces, -0.22, 0.18) if pieces else 1.0
    result = jax.random.normal(own_key, dims, jnp.float32) * width * level
    return jnp.minimum(jnp.maximum(result, -limit), limit).astype(held_as)


def setup_inputs(seed: int = 0) -> dict:
    key_of = jax.random.split(jax.random.key(seed), 7)
    query_proj = draw_query_proj(jax.random.fold_in(key_of[6], 71), 0)
    key_proj = draw_key_proj(jax.random.fold_in(key_of[6], 71), 0)
    value_proj = noise(key_of[2], (SEQ, D), 1.0, 6.0, ((0, 32),))
    attn_output = noise(key_of[3], (SEQ, D), 1.0, 6.0, ((0, 32),))
    out_grad = noise(key_of[4], (SEQ, D), 1.0, 6.0, ((0, 32),))
    random_blocks = draw_random_blocks(jax.random.fold_in(key_of[6], 71), 0)
    return dict(query_proj=query_proj, key_proj=key_proj, value_proj=value_proj, attn_output=attn_output, out_grad=out_grad, random_blocks=random_blocks)


def head_grads(tensors, random_blocks):
    query_rows, key_rows, value_rows, output_rows, grad_rows = tensors
    score_scale = HD ** -0.5
    extent = 3 + RAND
    query_blocks = query_rows.reshape(NB, BLOCK, HD)
    key_blocks = key_rows.reshape(NB, BLOCK, HD)
    value_blocks = value_rows.reshape(NB, BLOCK, HD)
    grad_blocks = grad_rows.reshape(NB, BLOCK, HD)
    row_delta = jnp.sum(output_rows.astype(jnp.float32) * grad_rows.astype(jnp.float32), axis=1).reshape(NB, BLOCK)
    block_ids = jnp.arange(NB, dtype=jnp.int32)
    listed = jnp.concatenate([block_ids[:, None], block_ids[:, None] - 1, jnp.zeros((NB, 1), jnp.int32), random_blocks.astype(jnp.int32)], axis=1)
    order = jnp.arange(extent, dtype=jnp.int32)
    earlier = order[None, :] < order[:, None]
    repeated = jnp.any((listed[:, :, None] == listed[:, None, :]) & earlier[None, :, :], axis=2)
    usable = (listed >= 0) & jnp.logical_not(repeated)
    within = jnp.arange(BLOCK, dtype=jnp.int32)

    def visit(accum, block):
        key_acc, value_acc = accum
        safe = jnp.maximum(listed[block], 0)
        keep = usable[block]
        key_sel = key_blocks[safe].reshape(extent * BLOCK, HD)
        value_sel = value_blocks[safe].reshape(extent * BLOCK, HD)
        query_blk = query_blocks[block]
        grad_blk = grad_blocks[block]
        scores = jnp.dot(query_blk, key_sel.T, preferred_element_type=jnp.float32) * score_scale
        query_pos = block * BLOCK + within
        key_pos = (safe[:, None] * BLOCK + within[None, :]).reshape(-1)
        allowed = jnp.repeat(keep, BLOCK)[None, :] & (key_pos[None, :] <= query_pos[:, None])
        row_max = jnp.max(jnp.where(allowed, scores, -1e30), axis=1)
        total = jnp.sum(jnp.where(allowed, jnp.exp(scores - row_max[:, None]), 0.0), axis=1)
        log_total = row_max + jnp.log(total)
        probs = jnp.where(allowed, jnp.exp(scores - log_total[:, None]), 0.0)
        prob_grad = jnp.dot(grad_blk, value_sel.T, preferred_element_type=jnp.float32)
        score_grad = (probs * (prob_grad - row_delta[block][:, None]) * score_scale).astype(jnp.bfloat16)
        query_part = jnp.dot(score_grad, key_sel, preferred_element_type=jnp.float32).astype(jnp.bfloat16)
        key_part = jnp.dot(score_grad.T, query_blk, preferred_element_type=jnp.float32).reshape(extent, BLOCK, HD)
        value_part = jnp.dot(probs.astype(jnp.bfloat16).T, grad_blk, preferred_element_type=jnp.float32).reshape(extent, BLOCK, HD)
        return (key_acc.at[safe].add(key_part), value_acc.at[safe].add(value_part)), query_part

    zeros_acc = jnp.zeros((NB, BLOCK, HD), jnp.float32)
    (key_acc, value_acc), query_parts = lax.scan(visit, (zeros_acc, zeros_acc), block_ids)
    return (query_parts.reshape(SEQ, HD), key_acc.reshape(SEQ, HD).astype(jnp.bfloat16), value_acc.reshape(SEQ, HD).astype(jnp.bfloat16))


def split_heads(tensor):
    return tensor.reshape(SEQ, HEADS, HD).transpose(1, 0, 2)


def join_heads(tensor):
    return tensor.transpose(1, 0, 2).reshape(SEQ, HEADS * HD)


def reference(query_proj, key_proj, value_proj, attn_output, out_grad, random_blocks):
    stacked = (split_heads(query_proj), split_heads(key_proj), split_heads(value_proj), split_heads(attn_output), split_heads(out_grad))

    def per_head(tensors):
        return head_grads(tensors, random_blocks)

    query_grad, key_grad, value_grad = lax.map(per_head, stacked)
    return join_heads(query_grad), join_heads(key_grad), join_heads(value_grad)
```

```python
import functools
import math

import jax
import jax.numpy as jnp
from jax import lax
from jax.experimental import pallas as pl
from jax.experimental.pallas import tpu as pltpu
from jax.sharding import PartitionSpec as P

HD = 128
BLOCK = 128
RAND = 3
CAP = 2


def named_table(random_blocks, per_shard):
    block_count = random_blocks.shape[0]
    shard_count = block_count // per_shard
    entries = random_blocks.reshape(shard_count, per_shard * RAND)
    block_ids = jnp.arange(block_count, dtype=jnp.int32)
    named = jnp.any(entries[:, :, None] == block_ids[None, None, :], axis=1)
    owner = block_ids // per_shard
    named = named & (owner[None, :] != jnp.arange(shard_count, dtype=jnp.int32)[:, None])
    grouped = named.reshape(shard_count, shard_count, per_shard).astype(jnp.int32)
    rank_in = jnp.cumsum(grouped, axis=2) - grouped
    return (grouped, rank_in)


def send_slots(grouped, rank_in, cycle_rank, per_shard):
    mine = lax.dynamic_index_in_dim(grouped, cycle_rank, 1, keepdims=False)
    mine_rank = lax.dynamic_index_in_dim(rank_in, cycle_rank, 1, keepdims=False)
    slot_ids = jnp.arange(CAP, dtype=jnp.int32)
    hit = (mine[:, None, :] == 1) & (mine_rank[:, None, :] == slot_ids[None, :, None])
    positions = jnp.arange(per_shard, dtype=jnp.int32)
    select = jnp.sum(jnp.where(hit, positions[None, None, :], 0), axis=2)
    filled = jnp.any(hit, axis=2)
    return (select, filled)


def on_device(query_proj, key_proj, value_proj, attn_output, out_grad, random_blocks):
    tok_count = query_proj.shape[0]
    head_count = query_proj.shape[1] // HD
    score_scale = HD ** (-0.5)
    extent = 3 + RAND

    def to_heads(tensor):
        return tensor.reshape(tok_count, head_count, HD)

    query_rows, key_rows, value_rows, output_rows, grad_rows = (
        lax.all_to_all(to_heads(query_proj), "uly", split_axis=1, concat_axis=0, tiled=True),
        lax.all_to_all(to_heads(key_proj), "uly", split_axis=1, concat_axis=0, tiled=True),
        lax.all_to_all(to_heads(value_proj), "uly", split_axis=1, concat_axis=0, tiled=True),
        lax.all_to_all(to_heads(attn_output), "uly", split_axis=1, concat_axis=0, tiled=True),
        lax.all_to_all(to_heads(out_grad), "uly", split_axis=1, concat_axis=0, tiled=True),
    )
    row_delta = jnp.sum(
        output_rows.astype(jnp.float32) * grad_rows.astype(jnp.float32), axis=2
    ).reshape(-1)
    shard_len = query_rows.shape[0]
    per_shard = shard_len // BLOCK
    query_blocks = query_rows.reshape(per_shard, BLOCK, HD)
    key_blocks = key_rows.reshape(per_shard, BLOCK, HD)
    value_blocks = value_rows.reshape(per_shard, BLOCK, HD)
    grad_blocks = grad_rows.reshape(per_shard, BLOCK, HD)
    delta_blocks = row_delta.reshape(per_shard, BLOCK)
    cycle_size = lax.axis_size("blk")
    cycle_rank = lax.axis_index("blk")
    block_count = random_blocks.shape[0]
    grouped, rank_in = named_table(random_blocks, per_shard)
    select, filled = send_slots(grouped, rank_in, cycle_rank, per_shard)
    key_send = jnp.where(
        filled[:, :, None, None],
        jnp.take(key_blocks, select.reshape(-1), axis=0).reshape(cycle_size, CAP, BLOCK, HD),
        jnp.zeros((), jnp.bfloat16),
    )
    value_send = jnp.where(
        filled[:, :, None, None],
        jnp.take(value_blocks, select.reshape(-1), axis=0).reshape(cycle_size, CAP, BLOCK, HD),
        jnp.zeros((), jnp.bfloat16),
    )
    extra_key = jnp.broadcast_to(
        jnp.stack([key_blocks[per_shard - 1], key_blocks[0]])[None], (cycle_size, 2, BLOCK, HD)
    )
    extra_value = jnp.broadcast_to(
        jnp.stack([value_blocks[per_shard - 1], value_blocks[0]])[None], (cycle_size, 2, BLOCK, HD)
    )
    all_key, all_value = (
        lax.all_to_all(
            jnp.concatenate([key_send, extra_key], axis=1),
            "blk",
            split_axis=0,
            concat_axis=0,
            tiled=True,
        ),
        lax.all_to_all(
            jnp.concatenate([value_send, extra_value], axis=1),
            "blk",
            split_axis=0,
            concat_axis=0,
            tiled=True,
        ),
    )
    far_key = all_key[:, :CAP]
    far_value = all_value[:, :CAP]
    before_rank = jnp.maximum(cycle_rank - 1, 0)
    prev_key = lax.dynamic_index_in_dim(all_key, before_rank, 0, keepdims=False)[CAP]
    prev_value = lax.dynamic_index_in_dim(all_value, before_rank, 0, keepdims=False)[CAP]
    first_key = all_key[0, CAP + 1]
    first_value = all_value[0, CAP + 1]
    key_store = jnp.concatenate(
        [key_blocks, prev_key[None], first_key[None], far_key.reshape(cycle_size * CAP, BLOCK, HD)],
        axis=0,
    )
    value_store = jnp.concatenate(
        [
            value_blocks,
            prev_value[None],
            first_value[None],
            far_value.reshape(cycle_size * CAP, BLOCK, HD),
        ],
        axis=0,
    )
    store_size = key_store.shape[0]
    picked = lax.dynamic_slice_in_dim(random_blocks, cycle_rank * per_shard, per_shard, 0)
    own_rank = lax.dynamic_index_in_dim(rank_in, cycle_rank, 0, keepdims=False).reshape(-1)
    all_ids = jnp.arange(block_count, dtype=jnp.int32)
    slot_of = jnp.sum(
        jnp.where(picked[:, :, None] == all_ids[None, None, :], own_rank[None, None, :], 0), axis=2
    )
    owner = picked // per_shard
    random_index = jnp.where(
        owner == cycle_rank, picked - cycle_rank * per_shard, per_shard + 2 + owner * CAP + slot_of
    )
    local_ids = jnp.arange(per_shard, dtype=jnp.int32)
    global_ids = cycle_rank * per_shard + local_ids
    listed = jnp.concatenate(
        [
            global_ids[:, None],
            global_ids[:, None] - 1,
            jnp.zeros((per_shard, 1), jnp.int32),
            picked,
        ],
        axis=1,
    )
    first_index = jnp.zeros((per_shard, 1), jnp.int32) + jnp.where(
        cycle_rank == 0, 0, per_shard + 1
    ).astype(jnp.int32)
    store_index = jnp.concatenate(
        [
            local_ids[:, None],
            jnp.where(local_ids >= 1, local_ids - 1, per_shard)[:, None],
            first_index,
            random_index,
        ],
        axis=1,
    )
    order = jnp.arange(extent, dtype=jnp.int32)
    earlier = order[None, :] < order[:, None]
    repeated = jnp.any((listed[:, :, None] == listed[:, None, :]) & earlier[None, :, :], axis=2)
    usable = (listed >= 0) & jnp.logical_not(repeated)
    within = jnp.arange(BLOCK, dtype=jnp.int32)
    group = math.gcd(per_shard, max(1, 512 // BLOCK))
    group_count = per_shard // group

    def group_turn(carry, group_index):
        key_grad_store, value_grad_store = carry
        first = group_index * group
        query_grp = lax.dynamic_slice_in_dim(query_blocks, first, group, 0)
        grad_grp = lax.dynamic_slice_in_dim(grad_blocks, first, group, 0)
        delta_grp = lax.dynamic_slice_in_dim(delta_blocks, first, group, 0)
        index_grp = lax.dynamic_slice_in_dim(store_index, first, group, 0).reshape(-1)
        listed_grp = lax.dynamic_slice_in_dim(listed, first, group, 0)
        usable_grp = lax.dynamic_slice_in_dim(usable, first, group, 0)
        key_sel = jnp.take(key_store, index_grp, axis=0).reshape(group, extent * BLOCK, HD)
        value_sel = jnp.take(value_store, index_grp, axis=0).reshape(group, extent * BLOCK, HD)
        scores = (
            jnp.einsum("gqd,gkd->gqk", query_grp, key_sel, preferred_element_type=jnp.float32)
            * score_scale
        )
        query_pos = (cycle_rank * per_shard + first + jnp.arange(group, dtype=jnp.int32))[
            :, None
        ] * BLOCK + within[None, :]
        key_pos = (listed_grp[:, :, None] * BLOCK + within[None, None, :]).reshape(
            group, extent * BLOCK
        )
        allowed = jnp.repeat(usable_grp, BLOCK, axis=1)[:, None, :] & (
            key_pos[:, None, :] <= query_pos[:, :, None]
        )
        row_max = jnp.max(jnp.where(allowed, scores, -1e30), axis=2)
        total = jnp.sum(jnp.where(allowed, jnp.exp(scores - row_max[:, :, None]), 0.0), axis=2)
        log_total = row_max + jnp.log(total)
        probs = jnp.where(allowed, jnp.exp(scores - log_total[:, :, None]), 0.0)
        prob_grad = jnp.einsum(
            "gqd,gkd->gqk", grad_grp, value_sel, preferred_element_type=jnp.float32
        )
        score_grad = (probs * (prob_grad - delta_grp[:, :, None]) * score_scale).astype(
            jnp.bfloat16
        )
        query_part = jnp.einsum(
            "gqk,gkd->gqd", score_grad, key_sel, preferred_element_type=jnp.float32
        ).astype(jnp.bfloat16)
        key_part = jnp.einsum(
            "gqk,gqd->gkd", score_grad, query_grp, preferred_element_type=jnp.float32
        )
        value_part = jnp.einsum(
            "gqk,gqd->gkd", probs.astype(jnp.bfloat16), grad_grp, preferred_element_type=jnp.float32
        )
        key_grad_store = key_grad_store.at[index_grp].add(
            key_part.reshape(group * extent, BLOCK, HD)
        )
        value_grad_store = value_grad_store.at[index_grp].add(
            value_part.reshape(group * extent, BLOCK, HD)
        )
        return ((key_grad_store, value_grad_store), query_part)

    zero_store = jnp.zeros((store_size, BLOCK, HD), jnp.float32)
    (key_grad_store, value_grad_store), query_parts = lax.scan(
        group_turn, (zero_store, zero_store), jnp.arange(group_count, dtype=jnp.int32)
    )
    query_acc = query_parts.reshape(shard_len, HD)
    key_acc = key_grad_store[:per_shard]
    value_acc = value_grad_store[:per_shard]
    far_key_grad = key_grad_store[per_shard + 2 :].reshape(cycle_size, CAP, BLOCK, HD)
    far_value_grad = value_grad_store[per_shard + 2 :].reshape(cycle_size, CAP, BLOCK, HD)
    dest_ids = jnp.arange(cycle_size, dtype=jnp.int32)
    to_prev = (dest_ids == cycle_rank - 1)[:, None, None]
    to_first = (dest_ids == 0)[:, None, None]
    extra_key_grad = jnp.stack(
        [
            jnp.where(to_prev, key_grad_store[per_shard][None], 0.0),
            jnp.where(to_first, key_grad_store[per_shard + 1][None], 0.0),
        ],
        axis=1,
    )
    extra_value_grad = jnp.stack(
        [
            jnp.where(to_prev, value_grad_store[per_shard][None], 0.0),
            jnp.where(to_first, value_grad_store[per_shard + 1][None], 0.0),
        ],
        axis=1,
    )
    all_key_back, all_value_back = (
        lax.all_to_all(
            jnp.concatenate([far_key_grad, extra_key_grad], axis=1),
            "blk",
            split_axis=0,
            concat_axis=0,
            tiled=True,
        ),
        lax.all_to_all(
            jnp.concatenate([far_value_grad, extra_value_grad], axis=1),
            "blk",
            split_axis=0,
            concat_axis=0,
            tiled=True,
        ),
    )
    back_key = all_key_back[:, :CAP]
    back_value = all_value_back[:, :CAP]
    prev_back = jnp.stack(
        [jnp.sum(all_key_back[:, CAP], axis=0), jnp.sum(all_value_back[:, CAP], axis=0)]
    )
    first_back = jnp.stack(
        [jnp.sum(all_key_back[:, CAP + 1], axis=0), jnp.sum(all_value_back[:, CAP + 1], axis=0)]
    )
    key_acc = key_acc.at[per_shard - 1].add(prev_back[0]).at[0].add(first_back[0])
    value_acc = value_acc.at[per_shard - 1].add(prev_back[1]).at[0].add(first_back[1])
    back_key = jnp.where(filled[:, :, None, None], back_key, 0.0).reshape(
        cycle_size * CAP, BLOCK, HD
    )
    back_value = jnp.where(filled[:, :, None, None], back_value, 0.0).reshape(
        cycle_size * CAP, BLOCK, HD
    )
    key_acc = key_acc.at[select.reshape(-1)].add(back_key).reshape(shard_len, HD)
    value_acc = value_acc.at[select.reshape(-1)].add(back_value).reshape(shard_len, HD)
    outgoing = (
        query_acc.reshape(shard_len, 1, HD),
        key_acc.astype(jnp.bfloat16).reshape(shard_len, 1, HD),
        value_acc.astype(jnp.bfloat16).reshape(shard_len, 1, HD),
    )
    query_back, key_back, value_back = (
        lax.all_to_all(outgoing[0], "uly", split_axis=0, concat_axis=1, tiled=True),
        lax.all_to_all(outgoing[1], "uly", split_axis=0, concat_axis=1, tiled=True),
        lax.all_to_all(outgoing[2], "uly", split_axis=0, concat_axis=1, tiled=True),
    )
    return (
        query_back.reshape(tok_count, head_count * HD),
        key_back.reshape(tok_count, head_count * HD),
        value_back.reshape(tok_count, head_count * HD),
    )


NEG = -1e30
KEY, QUERY, VALUE, GRAD = 0, 1, 2, 3
ROWS_BY_COLS = (((1,), (1,)), ((), ()))
COLS_BY_COLS = (((0,), (0,)), ((), ()))


def swing(count):
    offsets = [0]
    for step in range(1, count):
        offsets.append((step + 1) // 2 if step % 2 else count - step // 2)
    return offsets


def fused_kernel(
    shards,
    uly,
    picks_ref,
    q_ref,
    k_ref,
    v_ref,
    o_ref,
    g_ref,
    dq_ref,
    dk_ref,
    dv_ref,
    held,
    delta_send,
    delta_recv,
    bias,
    stats,
    scores,
    probs_low,
    score_grads,
    acc,
    outgoing,
    zs,
    zr,
    zl,
    ds_sem,
    dr_sem,
    fs,
    fr,
    ss,
    sr,
    os_sem,
    or_sem,
    ol,
):
    tok = q_ref.shape[0]
    length = tok * uly
    per = length // BLOCK
    gp = BLOCK // tok
    blocks = per * shards
    scale = HD ** (-0.5)
    b = lax.axis_index("blk")
    u = lax.axis_index("uly")
    inputs = {KEY: k_ref, QUERY: q_ref, VALUE: v_ref, GRAD: g_ref}
    f32 = jnp.float32

    def peer(step):
        return lax.rem(u + step, uly)

    def cols(p):
        return pl.ds(pl.multiple_of(p * HD, HD), HD)

    def rows(p):
        return pl.ds(pl.multiple_of(p * tok, tok), tok)

    def block_rows(c):
        return pl.ds(pl.multiple_of(c * BLOCK, BLOCK), BLOCK)

    def z_copy(t, p, sender):
        return pltpu.make_async_remote_copy(
            src_ref=inputs[t].at[:, cols(p)],
            dst_ref=held.at[t, b, rows(sender), :],
            send_sem=zs.at[t, p],
            recv_sem=zr.at[t, sender],
            device_id={"blk": b, "uly": p},
            device_id_type=pl.DeviceIdType.MESH,
        )

    def d_copy(p, sender):
        return pltpu.make_async_remote_copy(
            src_ref=delta_send.at[p],
            dst_ref=delta_recv.at[sender],
            send_sem=ds_sem.at[p],
            recv_sem=dr_sem.at[sender],
            device_id={"blk": b, "uly": p},
            device_id_type=pl.DeviceIdType.MESH,
        )

    def f_copy(t, c, to, sender):
        return pltpu.make_async_remote_copy(
            src_ref=held.at[t, sender, block_rows(c), :],
            dst_ref=held.at[t, sender, block_rows(c), :],
            send_sem=fs.at[t, c, to],
            recv_sem=fr.at[t, c, sender],
            device_id={"blk": to, "uly": u},
            device_id_type=pl.DeviceIdType.MESH,
        )

    def s_copy(to, sender):
        return pltpu.make_async_remote_copy(
            src_ref=stats.at[sender],
            dst_ref=stats.at[sender],
            send_sem=ss.at[to],
            recv_sem=sr.at[sender],
            device_id={"blk": to, "uly": u},
            device_id_type=pl.DeviceIdType.MESH,
        )

    results = (dq_ref, dk_ref, dv_ref)

    def o_copy(t, p, sender):
        return pltpu.make_async_remote_copy(
            src_ref=outgoing.at[t, rows(p), :],
            dst_ref=results[t].at[:, cols(sender)],
            send_sem=os_sem.at[t, p],
            recv_sem=or_sem.at[t, sender],
            device_id={"blk": b, "uly": p},
            device_id_type=pl.DeviceIdType.MESH,
        )

    def o_local(t):
        return pltpu.make_async_copy(
            outgoing.at[t, rows(u), :], results[t].at[:, cols(u)], ol.at[t]
        )

    def z_local(t):
        return pltpu.make_async_copy(inputs[t].at[:, cols(u)], held.at[t, b, rows(u), :], zl.at[t])

    barrier = pltpu.get_barrier_semaphore()
    for step in range(1, uly):
        pl.semaphore_signal(
            barrier,
            inc=1,
            device_id={"blk": b, "uly": peer(step)},
            device_id_type=pl.DeviceIdType.MESH,
        )
    for step in range(1, shards):
        pl.semaphore_signal(
            barrier,
            inc=1,
            device_id={"blk": lax.rem(b + step, shards), "uly": u},
            device_id_type=pl.DeviceIdType.MESH,
        )
    pl.semaphore_wait(barrier, uly - 1 + shards - 1)

    middle = uly // 2
    far_first = sorted(range(1, uly), key=lambda step: abs(step - middle))
    for t in (KEY, QUERY, VALUE, GRAD):
        for step in far_first:
            z_copy(t, peer(step), u).start()
        z_local(t).start()

    product = o_ref[...].astype(f32) * g_ref[...].astype(f32)
    high = product.astype(jnp.bfloat16)
    low = (product - high.astype(f32)).astype(jnp.bfloat16)
    head_of = lax.broadcasted_iota(jnp.int32, (uly, uly * HD), 1) // HD
    pick_head = jnp.where(
        head_of == lax.broadcasted_iota(jnp.int32, (uly, uly * HD), 0), 1.0, 0.0
    ).astype(jnp.bfloat16)
    sums = lax.dot_general(
        pick_head, jnp.concatenate([high] * gp, axis=0), ROWS_BY_COLS, preferred_element_type=f32
    ) + lax.dot_general(
        pick_head, jnp.concatenate([low] * gp, axis=0), ROWS_BY_COLS, preferred_element_type=f32
    )
    place = lax.broadcasted_iota(jnp.int32, (uly, BLOCK), 1) // tok
    sums = jnp.where(place == lax.rem(u, gp), sums, 0.0)
    for head in range(uly):
        delta_send[head] = sums[head : head + 1]
    for step in far_first:
        d_copy(peer(step), u).start()
    delta_recv[u] = delta_send[u]

    lane_block = lax.broadcasted_iota(jnp.int32, (1, length), 1) // BLOCK
    key_block = lax.broadcasted_iota(jnp.int32, (blocks, length), 0)
    for s in range(shards):
        query_block = lane_block + s * per
        hit = (key_block == query_block) | (key_block == query_block - 1) | (key_block == 0)
        for r in range(RAND):
            named = jnp.zeros((1, length), jnp.int32)
            for i in range(per):
                named = jnp.where(lane_block == i, picks_ref[s * per + i, r], named)
            hit = hit | (key_block == named)
        hit = hit & (key_block <= query_block)
        bias[s] = jnp.where(hit, 0.0, NEG)

    own_block = u // gp

    def forward(t):
        z_local(t).wait()
        for offset in swing(per):
            c = lax.rem(own_block + offset, per)
            for i in range(gp):
                p = c * gp + i

                @pl.when(p != u)
                def _():
                    z_copy(t, p, p).wait_recv()

            for to in range(shards):
                goes = (to > b) if t in (KEY, VALUE) else (to < b)

                @pl.when(goes)
                def _():
                    f_copy(t, c, to, b).start()

    def tile_scores(s_key, s_query, jb):
        keys = held[KEY, s_key, pl.ds(jb * BLOCK, BLOCK), :]
        tile = lax.dot_general(
            keys, held[QUERY, s_query], ROWS_BY_COLS, preferred_element_type=f32
        )
        return tile * scale + bias[s_query, pl.ds(s_key * per + jb, 1), :]

    forward(KEY)
    forward(QUERY)

    top = jnp.full((1, length), NEG, f32)
    for jb in range(per):
        tile = tile_scores(b, b, jb)
        key_at = lax.broadcasted_iota(jnp.int32, (BLOCK, length), 0) + jb * BLOCK
        query_at = lax.broadcasted_iota(jnp.int32, (BLOCK, length), 1)
        tile = jnp.where(key_at <= query_at, tile, NEG)
        scores[b, pl.ds(jb * BLOCK, BLOCK), :] = tile
        top = jnp.maximum(top, jnp.max(tile, axis=0, keepdims=True))

    forward(VALUE)
    forward(GRAD)

    def far_scores(s, top):
        for jb in range(per):
            f_copy(KEY, jb, b, s).wait_recv()
            tile = tile_scores(s, b, jb)
            scores[s, pl.ds(jb * BLOCK, BLOCK), :] = tile
            top = jnp.maximum(top, jnp.max(tile, axis=0, keepdims=True))
        return top

    top = lax.fori_loop(0, b, far_scores, top)

    def add_exp(s, total):
        for jb in range(per):
            tile = jnp.exp(scores[s, pl.ds(jb * BLOCK, BLOCK), :] - top)
            total = total + jnp.sum(tile, axis=0, keepdims=True)
        return total

    total = lax.fori_loop(0, b + 1, add_exp, jnp.zeros((1, length), f32))
    log_total = top + jnp.log(total)
    for step in range(1, uly):
        d_copy(peer(step), peer(step)).wait_recv()
    pieces = []
    for c in range(per):
        piece = delta_recv[c * gp]
        for i in range(1, gp):
            piece = piece + delta_recv[c * gp + i]
        pieces.append(piece)
    delta = jnp.concatenate(pieces, axis=1)
    stats[b, 0:1, :] = log_total
    stats[b, 1:2, :] = delta
    for to in range(shards):

        @pl.when(to < b)
        def _():
            s_copy(to, b).start()

    def tile_grads(tile, s_key, s_query, jb, log_row, delta_row):
        probs = jnp.exp(tile - log_row)
        values = held[VALUE, s_key, pl.ds(jb * BLOCK, BLOCK), :]
        prob_grad = lax.dot_general(
            values, held[GRAD, s_query], ROWS_BY_COLS, preferred_element_type=f32
        )
        grads = (probs * (prob_grad - delta_row) * scale).astype(jnp.bfloat16)
        return probs.astype(jnp.bfloat16), grads

    for jb in range(per):
        probs, grads = tile_grads(
            scores[b, pl.ds(jb * BLOCK, BLOCK), :], b, b, jb, log_total, delta
        )
        probs_low[pl.ds(jb * BLOCK, BLOCK), :] = probs
        score_grads[pl.ds(jb * BLOCK, BLOCK), :] = grads
    acc[0] = lax.dot_general(
        score_grads[...], held[KEY, b], COLS_BY_COLS, preferred_element_type=f32
    )
    acc[1] = jnp.dot(score_grads[...], held[QUERY, b], preferred_element_type=f32)
    acc[2] = jnp.dot(probs_low[...], held[GRAD, b], preferred_element_type=f32)

    def far_keys(s, carry):
        for jb in range(per):
            f_copy(VALUE, jb, b, s).wait_recv()
            _, grads = tile_grads(
                scores[s, pl.ds(jb * BLOCK, BLOCK), :], s, b, jb, log_total, delta
            )
            score_grads[pl.ds(jb * BLOCK, BLOCK), :] = grads
        acc[0] += lax.dot_general(
            score_grads[...], held[KEY, s], COLS_BY_COLS, preferred_element_type=f32
        )
        return carry

    lax.fori_loop(0, b, far_keys, 0)

    def send_result(t):
        outgoing[t] = acc[t].astype(jnp.bfloat16)
        for step in far_first:
            o_copy(t, peer(step), u).start()
        o_local(t).start()

    send_result(0)

    def far_queries(s, carry):
        for c in range(per):
            f_copy(QUERY, c, b, s).wait_recv()
            f_copy(GRAD, c, b, s).wait_recv()
        s_copy(b, s).wait_recv()
        log_row = stats[s, 0:1, :]
        delta_row = stats[s, 1:2, :]
        for jb in range(per):
            probs, grads = tile_grads(tile_scores(b, s, jb), b, s, jb, log_row, delta_row)
            probs_low[pl.ds(jb * BLOCK, BLOCK), :] = probs
            score_grads[pl.ds(jb * BLOCK, BLOCK), :] = grads
        acc[1] += jnp.dot(score_grads[...], held[QUERY, s], preferred_element_type=f32)
        acc[2] += jnp.dot(probs_low[...], held[GRAD, s], preferred_element_type=f32)
        return carry

    lax.fori_loop(b + 1, shards, far_queries, 0)
    send_result(1)
    send_result(2)

    for step in range(1, uly):
        p = peer(step)
        d_copy(p, u).wait_send()
        for t in (KEY, QUERY, VALUE, GRAD):
            z_copy(t, p, u).wait_send()
    for to in range(shards):

        @pl.when(to > b)
        def _():
            for c in range(per):
                f_copy(KEY, c, to, b).wait_send()
                f_copy(VALUE, c, to, b).wait_send()

        @pl.when(to < b)
        def _():
            for c in range(per):
                f_copy(QUERY, c, to, b).wait_send()
                f_copy(GRAD, c, to, b).wait_send()
            s_copy(to, b).wait_send()

    for t in range(3):
        o_local(t).wait()
        for step in range(1, uly):
            p = peer(step)
            o_copy(t, p, p).wait_recv()
            o_copy(t, p, u).wait_send()


def fused_on_device(shards, uly, q, k, v, o, g, random_blocks):
    tok, width = q.shape
    length = tok * uly
    per = length // BLOCK
    dma = pltpu.SemaphoreType.DMA
    vmem = pl.BlockSpec(memory_space=pltpu.VMEM)
    return pl.pallas_call(
        functools.partial(fused_kernel, shards, uly),
        out_shape=[jax.ShapeDtypeStruct((tok, width), jnp.bfloat16)] * 3,
        in_specs=[pl.BlockSpec(memory_space=pltpu.SMEM)] + [vmem] * 5,
        out_specs=[vmem] * 3,
        scratch_shapes=[
            pltpu.VMEM((4, shards, length, HD), jnp.bfloat16),
            pltpu.VMEM((uly, 1, BLOCK), jnp.float32),
            pltpu.VMEM((uly, 1, BLOCK), jnp.float32),
            pltpu.VMEM((shards, shards * per, length), jnp.float32),
            pltpu.VMEM((shards, 2, length), jnp.float32),
            pltpu.VMEM((shards, length, length), jnp.float32),
            pltpu.VMEM((length, length), jnp.bfloat16),
            pltpu.VMEM((length, length), jnp.bfloat16),
            pltpu.VMEM((3, length, HD), jnp.float32),
            pltpu.VMEM((3, length, HD), jnp.bfloat16),
            dma((4, uly)),
            dma((4, uly)),
            dma((4,)),
            dma((uly,)),
            dma((uly,)),
            dma((4, per, shards)),
            dma((4, per, shards)),
            dma((shards,)),
            dma((shards,)),
            dma((3, uly)),
            dma((3, uly)),
            dma((3,)),
        ],
        compiler_params=pltpu.CompilerParams(
            collective_id=0, has_side_effects=True, vmem_limit_bytes=40 * 1024 * 1024
        ),
    )(random_blocks, q, k, v, o, g)


def wide_or_fused(shards, uly, *operands):
    tok, width = operands[0].shape
    length = tok * uly
    fits = shards * length * length * 4 <= 16 * 1024 * 1024
    if fits and width == uly * HD and BLOCK % tok == 0 and length % BLOCK == 0:
        return tuple(fused_on_device(shards, uly, *operands))
    return on_device(*operands)


def solution(mesh):
    return jax.shard_map(
        functools.partial(wide_or_fused, mesh.shape["blk"], mesh.shape["uly"]),
        mesh=mesh,
        in_specs=(
            P(("blk", "uly"), None),
            P(("blk", "uly"), None),
            P(("blk", "uly"), None),
            P(("blk", "uly"), None),
            P(("blk", "uly"), None),
            P(),
        ),
        out_specs=(P(("blk", "uly"), None), P(("blk", "uly"), None), P(("blk", "uly"), None)),
        check_vma=False,
    )
```

```python
import functools
import math

import jax
import jax.numpy as jnp
from jax import lax
from jax.experimental import pallas as pl
from jax.experimental.pallas import tpu as pltpu
from jax.sharding import PartitionSpec as P

HD = 128
BLOCK = 128
RAND = 3
CAP = 2


def named_table(random_blocks, per_shard):
    block_count = random_blocks.shape[0]
    shard_count = block_count // per_shard
    entries = random_blocks.reshape(shard_count, per_shard * RAND)
    block_ids = jnp.arange(block_count, dtype=jnp.int32)
    named = jnp.any(entries[:, :, None] == block_ids[None, None, :], axis=1)
    owner = block_ids // per_shard
    named = named & (owner[None, :] != jnp.arange(shard_count, dtype=jnp.int32)[:, None])
    grouped = named.reshape(shard_count, shard_count, per_shard).astype(jnp.int32)
    rank_in = jnp.cumsum(grouped, axis=2) - grouped
    return (grouped, rank_in)


def send_slots(grouped, rank_in, cycle_rank, per_shard):
    mine = lax.dynamic_index_in_dim(grouped, cycle_rank, 1, keepdims=False)
    mine_rank = lax.dynamic_index_in_dim(rank_in, cycle_rank, 1, keepdims=False)
    slot_ids = jnp.arange(CAP, dtype=jnp.int32)
    hit = (mine[:, None, :] == 1) & (mine_rank[:, None, :] == slot_ids[None, :, None])
    positions = jnp.arange(per_shard, dtype=jnp.int32)
    select = jnp.sum(jnp.where(hit, positions[None, None, :], 0), axis=2)
    filled = jnp.any(hit, axis=2)
    return (select, filled)


def on_device(query_proj, key_proj, value_proj, attn_output, out_grad, random_blocks):
    tok_count = query_proj.shape[0]
    head_count = query_proj.shape[1] // HD
    score_scale = HD ** (-0.5)
    extent = 3 + RAND

    def to_heads(tensor):
        return tensor.reshape(tok_count, head_count, HD)

    query_rows, key_rows, value_rows, output_rows, grad_rows = (
        lax.all_to_all(to_heads(query_proj), "uly", split_axis=1, concat_axis=0, tiled=True),
        lax.all_to_all(to_heads(key_proj), "uly", split_axis=1, concat_axis=0, tiled=True),
        lax.all_to_all(to_heads(value_proj), "uly", split_axis=1, concat_axis=0, tiled=True),
        lax.all_to_all(to_heads(attn_output), "uly", split_axis=1, concat_axis=0, tiled=True),
        lax.all_to_all(to_heads(out_grad), "uly", split_axis=1, concat_axis=0, tiled=True),
    )
    row_delta = jnp.sum(
        output_rows.astype(jnp.float32) * grad_rows.astype(jnp.float32), axis=2
    ).reshape(-1)
    shard_len = query_rows.shape[0]
    per_shard = shard_len // BLOCK
    query_blocks = query_rows.reshape(per_shard, BLOCK, HD)
    key_blocks = key_rows.reshape(per_shard, BLOCK, HD)
    value_blocks = value_rows.reshape(per_shard, BLOCK, HD)
    grad_blocks = grad_rows.reshape(per_shard, BLOCK, HD)
    delta_blocks = row_delta.reshape(per_shard, BLOCK)
    cycle_size = lax.axis_size("blk")
    cycle_rank = lax.axis_index("blk")
    block_count = random_blocks.shape[0]
    grouped, rank_in = named_table(random_blocks, per_shard)
    select, filled = send_slots(grouped, rank_in, cycle_rank, per_shard)
    key_send = jnp.where(
        filled[:, :, None, None],
        jnp.take(key_blocks, select.reshape(-1), axis=0).reshape(cycle_size, CAP, BLOCK, HD),
        jnp.zeros((), jnp.bfloat16),
    )
    value_send = jnp.where(
        filled[:, :, None, None],
        jnp.take(value_blocks, select.reshape(-1), axis=0).reshape(cycle_size, CAP, BLOCK, HD),
        jnp.zeros((), jnp.bfloat16),
    )
    extra_key = jnp.broadcast_to(
        jnp.stack([key_blocks[per_shard - 1], key_blocks[0]])[None], (cycle_size, 2, BLOCK, HD)
    )
    extra_value = jnp.broadcast_to(
        jnp.stack([value_blocks[per_shard - 1], value_blocks[0]])[None], (cycle_size, 2, BLOCK, HD)
    )
    all_key, all_value = (
        lax.all_to_all(
            jnp.concatenate([key_send, extra_key], axis=1),
            "blk",
            split_axis=0,
            concat_axis=0,
            tiled=True,
        ),
        lax.all_to_all(
            jnp.concatenate([value_send, extra_value], axis=1),
            "blk",
            split_axis=0,
            concat_axis=0,
            tiled=True,
        ),
    )
    far_key = all_key[:, :CAP]
    far_value = all_value[:, :CAP]
    before_rank = jnp.maximum(cycle_rank - 1, 0)
    prev_key = lax.dynamic_index_in_dim(all_key, before_rank, 0, keepdims=False)[CAP]
    prev_value = lax.dynamic_index_in_dim(all_value, before_rank, 0, keepdims=False)[CAP]
    first_key = all_key[0, CAP + 1]
    first_value = all_value[0, CAP + 1]
    key_store = jnp.concatenate(
        [key_blocks, prev_key[None], first_key[None], far_key.reshape(cycle_size * CAP, BLOCK, HD)],
        axis=0,
    )
    value_store = jnp.concatenate(
        [
            value_blocks,
            prev_value[None],
            first_value[None],
            far_value.reshape(cycle_size * CAP, BLOCK, HD),
        ],
        axis=0,
    )
    store_size = key_store.shape[0]
    picked = lax.dynamic_slice_in_dim(random_blocks, cycle_rank * per_shard, per_shard, 0)
    own_rank = lax.dynamic_index_in_dim(rank_in, cycle_rank, 0, keepdims=False).reshape(-1)
    all_ids = jnp.arange(block_count, dtype=jnp.int32)
    slot_of = jnp.sum(
        jnp.where(picked[:, :, None] == all_ids[None, None, :], own_rank[None, None, :], 0), axis=2
    )
    owner = picked // per_shard
    random_index = jnp.where(
        owner == cycle_rank, picked - cycle_rank * per_shard, per_shard + 2 + owner * CAP + slot_of
    )
    local_ids = jnp.arange(per_shard, dtype=jnp.int32)
    global_ids = cycle_rank * per_shard + local_ids
    listed = jnp.concatenate(
        [
            global_ids[:, None],
            global_ids[:, None] - 1,
            jnp.zeros((per_shard, 1), jnp.int32),
            picked,
        ],
        axis=1,
    )
    first_index = jnp.zeros((per_shard, 1), jnp.int32) + jnp.where(
        cycle_rank == 0, 0, per_shard + 1
    ).astype(jnp.int32)
    store_index = jnp.concatenate(
        [
            local_ids[:, None],
            jnp.where(local_ids >= 1, local_ids - 1, per_shard)[:, None],
            first_index,
            random_index,
        ],
        axis=1,
    )
    order = jnp.arange(extent, dtype=jnp.int32)
    earlier = order[None, :] < order[:, None]
    repeated = jnp.any((listed[:, :, None] == listed[:, None, :]) & earlier[None, :, :], axis=2)
    usable = (listed >= 0) & jnp.logical_not(repeated)
    within = jnp.arange(BLOCK, dtype=jnp.int32)
    group = math.gcd(per_shard, max(1, 512 // BLOCK))
    group_count = per_shard // group

    def group_turn(carry, group_index):
        key_grad_store, value_grad_store = carry
        first = group_index * group
        query_grp = lax.dynamic_slice_in_dim(query_blocks, first, group, 0)
        grad_grp = lax.dynamic_slice_in_dim(grad_blocks, first, group, 0)
        delta_grp = lax.dynamic_slice_in_dim(delta_blocks, first, group, 0)
        index_grp = lax.dynamic_slice_in_dim(store_index, first, group, 0).reshape(-1)
        listed_grp = lax.dynamic_slice_in_dim(listed, first, group, 0)
        usable_grp = lax.dynamic_slice_in_dim(usable, first, group, 0)
        key_sel = jnp.take(key_store, index_grp, axis=0).reshape(group, extent * BLOCK, HD)
        value_sel = jnp.take(value_store, index_grp, axis=0).reshape(group, extent * BLOCK, HD)
        scores = (
            jnp.einsum("gqd,gkd->gqk", query_grp, key_sel, preferred_element_type=jnp.float32)
            * score_scale
        )
        query_pos = (cycle_rank * per_shard + first + jnp.arange(group, dtype=jnp.int32))[
            :, None
        ] * BLOCK + within[None, :]
        key_pos = (listed_grp[:, :, None] * BLOCK + within[None, None, :]).reshape(
            group, extent * BLOCK
        )
        allowed = jnp.repeat(usable_grp, BLOCK, axis=1)[:, None, :] & (
            key_pos[:, None, :] <= query_pos[:, :, None]
        )
        row_max = jnp.max(jnp.where(allowed, scores, -1e30), axis=2)
        total = jnp.sum(jnp.where(allowed, jnp.exp(scores - row_max[:, :, None]), 0.0), axis=2)
        log_total = row_max + jnp.log(total)
        probs = jnp.where(allowed, jnp.exp(scores - log_total[:, :, None]), 0.0)
        prob_grad = jnp.einsum(
            "gqd,gkd->gqk", grad_grp, value_sel, preferred_element_type=jnp.float32
        )
        score_grad = (probs * (prob_grad - delta_grp[:, :, None]) * score_scale).astype(
            jnp.bfloat16
        )
        query_part = jnp.einsum(
            "gqk,gkd->gqd", score_grad, key_sel, preferred_element_type=jnp.float32
        ).astype(jnp.bfloat16)
        key_part = jnp.einsum(
            "gqk,gqd->gkd", score_grad, query_grp, preferred_element_type=jnp.float32
        )
        value_part = jnp.einsum(
            "gqk,gqd->gkd", probs.astype(jnp.bfloat16), grad_grp, preferred_element_type=jnp.float32
        )
        key_grad_store = key_grad_store.at[index_grp].add(
            key_part.reshape(group * extent, BLOCK, HD)
        )
        value_grad_store = value_grad_store.at[index_grp].add(
            value_part.reshape(group * extent, BLOCK, HD)
        )
        return ((key_grad_store, value_grad_store), query_part)

    zero_store = jnp.zeros((store_size, BLOCK, HD), jnp.float32)
    (key_grad_store, value_grad_store), query_parts = lax.scan(
        group_turn, (zero_store, zero_store), jnp.arange(group_count, dtype=jnp.int32)
    )
    query_acc = query_parts.reshape(shard_len, HD)
    key_acc = key_grad_store[:per_shard]
    value_acc = value_grad_store[:per_shard]
    far_key_grad = key_grad_store[per_shard + 2 :].reshape(cycle_size, CAP, BLOCK, HD)
    far_value_grad = value_grad_store[per_shard + 2 :].reshape(cycle_size, CAP, BLOCK, HD)
    dest_ids = jnp.arange(cycle_size, dtype=jnp.int32)
    to_prev = (dest_ids == cycle_rank - 1)[:, None, None]
    to_first = (dest_ids == 0)[:, None, None]
    extra_key_grad = jnp.stack(
        [
            jnp.where(to_prev, key_grad_store[per_shard][None], 0.0),
            jnp.where(to_first, key_grad_store[per_shard + 1][None], 0.0),
        ],
        axis=1,
    )
    extra_value_grad = jnp.stack(
        [
            jnp.where(to_prev, value_grad_store[per_shard][None], 0.0),
            jnp.where(to_first, value_grad_store[per_shard + 1][None], 0.0),
        ],
        axis=1,
    )
    all_key_back, all_value_back = (
        lax.all_to_all(
            jnp.concatenate([far_key_grad, extra_key_grad], axis=1),
            "blk",
            split_axis=0,
            concat_axis=0,
            tiled=True,
        ),
        lax.all_to_all(
            jnp.concatenate([far_value_grad, extra_value_grad], axis=1),
            "blk",
            split_axis=0,
            concat_axis=0,
            tiled=True,
        ),
    )
    back_key = all_key_back[:, :CAP]
    back_value = all_value_back[:, :CAP]
    prev_back = jnp.stack(
        [jnp.sum(all_key_back[:, CAP], axis=0), jnp.sum(all_value_back[:, CAP], axis=0)]
    )
    first_back = jnp.stack(
        [jnp.sum(all_key_back[:, CAP + 1], axis=0), jnp.sum(all_value_back[:, CAP + 1], axis=0)]
    )
    key_acc = key_acc.at[per_shard - 1].add(prev_back[0]).at[0].add(first_back[0])
    value_acc = value_acc.at[per_shard - 1].add(prev_back[1]).at[0].add(first_back[1])
    back_key = jnp.where(filled[:, :, None, None], back_key, 0.0).reshape(
        cycle_size * CAP, BLOCK, HD
    )
    back_value = jnp.where(filled[:, :, None, None], back_value, 0.0).reshape(
        cycle_size * CAP, BLOCK, HD
    )
    key_acc = key_acc.at[select.reshape(-1)].add(back_key).reshape(shard_len, HD)
    value_acc = value_acc.at[select.reshape(-1)].add(back_value).reshape(shard_len, HD)
    outgoing = (
        query_acc.reshape(shard_len, 1, HD),
        key_acc.astype(jnp.bfloat16).reshape(shard_len, 1, HD),
        value_acc.astype(jnp.bfloat16).reshape(shard_len, 1, HD),
    )
    query_back, key_back, value_back = (
        lax.all_to_all(outgoing[0], "uly", split_axis=0, concat_axis=1, tiled=True),
        lax.all_to_all(outgoing[1], "uly", split_axis=0, concat_axis=1, tiled=True),
        lax.all_to_all(outgoing[2], "uly", split_axis=0, concat_axis=1, tiled=True),
    )
    return (
        query_back.reshape(tok_count, head_count * HD),
        key_back.reshape(tok_count, head_count * HD),
        value_back.reshape(tok_count, head_count * HD),
    )


NEG = -1e30
KEY, QUERY, VALUE, GRAD = 0, 1, 2, 3
ROWS_BY_COLS = (((1,), (1,)), ((), ()))
COLS_BY_COLS = (((0,), (0,)), ((), ()))


def swing(count):
    offsets = [0]
    for step in range(1, count):
        offsets.append((step + 1) // 2 if step % 2 else count - step // 2)
    return offsets


def fused_kernel(
    shards,
    uly,
    picks_ref,
    q_ref,
    k_ref,
    v_ref,
    o_ref,
    g_ref,
    dq_ref,
    dk_ref,
    dv_ref,
    rows_in,
    held,
    delta_send,
    delta_recv,
    bias,
    stats,
    scores,
    probs_low,
    score_grads,
    acc,
    outgoing,
    zs,
    zr,
    zl,
    ds_sem,
    dr_sem,
    fs,
    fr,
    ss,
    sr,
    os_sem,
    or_sem,
    ol,
    il,
):
    tok = q_ref.shape[0]
    length = tok * uly
    per = length // BLOCK
    gp = BLOCK // tok
    blocks = per * shards
    scale = HD ** (-0.5)
    b = lax.axis_index("blk")
    u = lax.axis_index("uly")
    inputs = {KEY: k_ref, QUERY: q_ref, VALUE: v_ref, GRAD: g_ref}
    f32 = jnp.float32

    def peer(step):
        return lax.rem(u + step, uly)

    def cols(p):
        return pl.ds(pl.multiple_of(p * HD, HD), HD)

    def rows(p):
        return pl.ds(pl.multiple_of(p * tok, tok), tok)

    def block_rows(c):
        return pl.ds(pl.multiple_of(c * BLOCK, BLOCK), BLOCK)

    def z_copy(t, p, sender):
        return pltpu.make_async_remote_copy(
            src_ref=inputs[t].at[:, cols(p)],
            dst_ref=held.at[t, b, rows(sender), :],
            send_sem=zs.at[t, p],
            recv_sem=zr.at[t, sender],
            device_id={"blk": b, "uly": p},
            device_id_type=pl.DeviceIdType.MESH,
        )

    def d_copy(p, sender):
        return pltpu.make_async_remote_copy(
            src_ref=delta_send.at[p],
            dst_ref=delta_recv.at[sender],
            send_sem=ds_sem.at[p],
            recv_sem=dr_sem.at[sender],
            device_id={"blk": b, "uly": p},
            device_id_type=pl.DeviceIdType.MESH,
        )

    def f_copy(t, c, to, sender):
        return pltpu.make_async_remote_copy(
            src_ref=held.at[t, sender, block_rows(c), :],
            dst_ref=held.at[t, sender, block_rows(c), :],
            send_sem=fs.at[t, c, to],
            recv_sem=fr.at[t, c, sender],
            device_id={"blk": to, "uly": u},
            device_id_type=pl.DeviceIdType.MESH,
        )

    def s_copy(to, sender):
        return pltpu.make_async_remote_copy(
            src_ref=stats.at[sender],
            dst_ref=stats.at[sender],
            send_sem=ss.at[to],
            recv_sem=sr.at[sender],
            device_id={"blk": to, "uly": u},
            device_id_type=pl.DeviceIdType.MESH,
        )

    results = (dq_ref, dk_ref, dv_ref)

    def o_copy(t, p, sender):
        return pltpu.make_async_remote_copy(
            src_ref=outgoing.at[t, rows(p), :],
            dst_ref=results[t].at[:, cols(sender)],
            send_sem=os_sem.at[t, p],
            recv_sem=or_sem.at[t, sender],
            device_id={"blk": b, "uly": p},
            device_id_type=pl.DeviceIdType.MESH,
        )

    def o_local(t):
        return pltpu.make_async_copy(
            outgoing.at[t, rows(u), :], results[t].at[:, cols(u)], ol.at[t]
        )

    def z_local(t):
        return pltpu.make_async_copy(inputs[t].at[:, cols(u)], held.at[t, b, rows(u), :], zl.at[t])

    fetches = (
        pltpu.make_async_copy(o_ref, rows_in.at[0], il.at[0]),
        pltpu.make_async_copy(g_ref, rows_in.at[1], il.at[1]),
    )
    for fetch in fetches:
        fetch.start()
    barrier = pltpu.get_barrier_semaphore()
    for step in range(1, uly):
        pl.semaphore_signal(
            barrier,
            inc=1,
            device_id={"blk": b, "uly": peer(step)},
            device_id_type=pl.DeviceIdType.MESH,
        )
    for step in range(1, shards):
        pl.semaphore_signal(
            barrier,
            inc=1,
            device_id={"blk": lax.rem(b + step, shards), "uly": u},
            device_id_type=pl.DeviceIdType.MESH,
        )
    pl.semaphore_wait(barrier, uly - 1 + shards - 1)

    middle = uly // 2
    far_first = sorted(range(1, uly), key=lambda step: abs(step - middle))
    for t in (KEY, QUERY, VALUE, GRAD):
        for step in far_first:
            z_copy(t, peer(step), u).start()
        z_local(t).start()

    for fetch in fetches:
        fetch.wait()
    product = rows_in[0].astype(f32) * rows_in[1].astype(f32)
    high = product.astype(jnp.bfloat16)
    low = (product - high.astype(f32)).astype(jnp.bfloat16)
    head_of = lax.broadcasted_iota(jnp.int32, (uly, uly * HD), 1) // HD
    pick_head = jnp.where(
        head_of == lax.broadcasted_iota(jnp.int32, (uly, uly * HD), 0), 1.0, 0.0
    ).astype(jnp.bfloat16)
    sums = lax.dot_general(
        pick_head, jnp.concatenate([high] * gp, axis=0), ROWS_BY_COLS, preferred_element_type=f32
    ) + lax.dot_general(
        pick_head, jnp.concatenate([low] * gp, axis=0), ROWS_BY_COLS, preferred_element_type=f32
    )
    place = lax.broadcasted_iota(jnp.int32, (uly, BLOCK), 1) // tok
    sums = jnp.where(place == lax.rem(u, gp), sums, 0.0)
    for head in range(uly):
        delta_send[head] = sums[head : head + 1]
    for step in far_first:
        d_copy(peer(step), u).start()
    delta_recv[u] = delta_send[u]

    lane_block = lax.broadcasted_iota(jnp.int32, (1, length), 1) // BLOCK
    key_block = lax.broadcasted_iota(jnp.int32, (blocks, length), 0)
    for s in range(shards):
        query_block = lane_block + s * per
        hit = (key_block == query_block) | (key_block == query_block - 1) | (key_block == 0)
        for r in range(RAND):
            named = jnp.zeros((1, length), jnp.int32)
            for i in range(per):
                named = jnp.where(lane_block == i, picks_ref[r, s * per + i], named)
            hit = hit | (key_block == named)
        hit = hit & (key_block <= query_block)
        bias[s] = jnp.where(hit, 0.0, NEG)

    own_block = u // gp

    def forward(t):
        z_local(t).wait()
        for offset in swing(per):
            c = lax.rem(own_block + offset, per)
            for i in range(gp):
                p = c * gp + i

                @pl.when(p != u)
                def _():
                    z_copy(t, p, p).wait_recv()

            for to in range(shards):
                goes = (to > b) if t in (KEY, VALUE) else (to < b)

                @pl.when(goes)
                def _():
                    f_copy(t, c, to, b).start()

    def tile_scores(s_key, s_query, jb):
        keys = held[KEY, s_key, pl.ds(jb * BLOCK, BLOCK), :]
        tile = lax.dot_general(
            keys, held[QUERY, s_query], ROWS_BY_COLS, preferred_element_type=f32
        )
        return tile * scale + bias[s_query, pl.ds(s_key * per + jb, 1), :]

    forward(KEY)
    forward(QUERY)

    top = jnp.full((1, length), NEG, f32)
    for jb in range(per):
        tile = tile_scores(b, b, jb)
        key_at = lax.broadcasted_iota(jnp.int32, (BLOCK, length), 0) + jb * BLOCK
        query_at = lax.broadcasted_iota(jnp.int32, (BLOCK, length), 1)
        tile = jnp.where(key_at <= query_at, tile, NEG)
        scores[b, pl.ds(jb * BLOCK, BLOCK), :] = tile
        top = jnp.maximum(top, jnp.max(tile, axis=0, keepdims=True))

    forward(VALUE)
    forward(GRAD)

    def far_scores(s, top):
        for jb in range(per):
            f_copy(KEY, jb, b, s).wait_recv()
            tile = tile_scores(s, b, jb)
            scores[s, pl.ds(jb * BLOCK, BLOCK), :] = tile
            top = jnp.maximum(top, jnp.max(tile, axis=0, keepdims=True))
        return top

    top = lax.fori_loop(0, b, far_scores, top)

    def add_exp(s, total):
        for jb in range(per):
            tile = jnp.exp(scores[s, pl.ds(jb * BLOCK, BLOCK), :] - top)
            total = total + jnp.sum(tile, axis=0, keepdims=True)
        return total

    total = lax.fori_loop(0, b + 1, add_exp, jnp.zeros((1, length), f32))
    log_total = top + jnp.log(total)
    for step in range(1, uly):
        d_copy(peer(step), peer(step)).wait_recv()
    pieces = []
    for c in range(per):
        piece = delta_recv[c * gp]
        for i in range(1, gp):
            piece = piece + delta_recv[c * gp + i]
        pieces.append(piece)
    delta = jnp.concatenate(pieces, axis=1)
    stats[b, 0:1, :] = log_total
    stats[b, 1:2, :] = delta
    for to in range(shards):

        @pl.when(to < b)
        def _():
            s_copy(to, b).start()

    def tile_grads(tile, s_key, s_query, jb, log_row, delta_row):
        probs = jnp.exp(tile - log_row)
        values = held[VALUE, s_key, pl.ds(jb * BLOCK, BLOCK), :]
        prob_grad = lax.dot_general(
            values, held[GRAD, s_query], ROWS_BY_COLS, preferred_element_type=f32
        )
        grads = (probs * (prob_grad - delta_row) * scale).astype(jnp.bfloat16)
        return probs.astype(jnp.bfloat16), grads

    for jb in range(per):
        probs, grads = tile_grads(
            scores[b, pl.ds(jb * BLOCK, BLOCK), :], b, b, jb, log_total, delta
        )
        probs_low[pl.ds(jb * BLOCK, BLOCK), :] = probs
        score_grads[pl.ds(jb * BLOCK, BLOCK), :] = grads
    acc[0] = lax.dot_general(
        score_grads[...], held[KEY, b], COLS_BY_COLS, preferred_element_type=f32
    )
    acc[1] = jnp.dot(score_grads[...], held[QUERY, b], preferred_element_type=f32)
    acc[2] = jnp.dot(probs_low[...], held[GRAD, b], preferred_element_type=f32)

    def far_keys(s, carry):
        for jb in range(per):
            f_copy(VALUE, jb, b, s).wait_recv()
            _, grads = tile_grads(
                scores[s, pl.ds(jb * BLOCK, BLOCK), :], s, b, jb, log_total, delta
            )
            score_grads[pl.ds(jb * BLOCK, BLOCK), :] = grads
        acc[0] += lax.dot_general(
            score_grads[...], held[KEY, s], COLS_BY_COLS, preferred_element_type=f32
        )
        return carry

    lax.fori_loop(0, b, far_keys, 0)

    def send_result(t):
        outgoing[t] = acc[t].astype(jnp.bfloat16)
        for step in far_first:
            o_copy(t, peer(step), u).start()
        o_local(t).start()

    send_result(0)

    def far_queries(s, carry):
        for c in range(per):
            f_copy(QUERY, c, b, s).wait_recv()
            f_copy(GRAD, c, b, s).wait_recv()
        s_copy(b, s).wait_recv()
        log_row = stats[s, 0:1, :]
        delta_row = stats[s, 1:2, :]
        for jb in range(per):
            probs, grads = tile_grads(tile_scores(b, s, jb), b, s, jb, log_row, delta_row)
            probs_low[pl.ds(jb * BLOCK, BLOCK), :] = probs
            score_grads[pl.ds(jb * BLOCK, BLOCK), :] = grads
        acc[1] += jnp.dot(score_grads[...], held[QUERY, s], preferred_element_type=f32)
        acc[2] += jnp.dot(probs_low[...], held[GRAD, s], preferred_element_type=f32)
        return carry

    lax.fori_loop(b + 1, shards, far_queries, 0)
    send_result(1)
    send_result(2)

    for step in range(1, uly):
        p = peer(step)
        d_copy(p, u).wait_send()
        for t in (KEY, QUERY, VALUE, GRAD):
            z_copy(t, p, u).wait_send()
    for to in range(shards):

        @pl.when(to > b)
        def _():
            for c in range(per):
                f_copy(KEY, c, to, b).wait_send()
                f_copy(VALUE, c, to, b).wait_send()

        @pl.when(to < b)
        def _():
            for c in range(per):
                f_copy(QUERY, c, to, b).wait_send()
                f_copy(GRAD, c, to, b).wait_send()
            s_copy(to, b).wait_send()

    for t in range(3):
        o_local(t).wait()
        for step in range(1, uly):
            p = peer(step)
            o_copy(t, p, p).wait_recv()
            o_copy(t, p, u).wait_send()


def write_out(a_ref, b_ref, c_ref, a_out, b_out, c_out):
    a_out[...] = a_ref[...]
    b_out[...] = b_ref[...]
    c_out[...] = c_ref[...]


def fused_on_device(shards, uly, q, k, v, o, g, random_blocks):
    tok, width = q.shape
    length = tok * uly
    per = length // BLOCK
    dma = pltpu.SemaphoreType.DMA
    hbm = pl.BlockSpec(memory_space=pltpu.HBM)
    results = pl.pallas_call(
        functools.partial(fused_kernel, shards, uly),
        out_shape=[jax.ShapeDtypeStruct((tok, width), jnp.bfloat16)] * 3,
        in_specs=[pl.BlockSpec(memory_space=pltpu.SMEM)] + [hbm] * 5,
        out_specs=[hbm] * 3,
        scratch_shapes=[
            pltpu.VMEM((2, tok, width), jnp.bfloat16),
            pltpu.VMEM((4, shards, length, HD), jnp.bfloat16),
            pltpu.VMEM((uly, 1, BLOCK), jnp.float32),
            pltpu.VMEM((uly, 1, BLOCK), jnp.float32),
            pltpu.VMEM((shards, shards * per, length), jnp.float32),
            pltpu.VMEM((shards, 2, length), jnp.float32),
            pltpu.VMEM((shards, length, length), jnp.float32),
            pltpu.VMEM((length, length), jnp.bfloat16),
            pltpu.VMEM((length, length), jnp.bfloat16),
            pltpu.VMEM((3, length, HD), jnp.float32),
            pltpu.VMEM((3, length, HD), jnp.bfloat16),
            dma((4, uly)),
            dma((4, uly)),
            dma((4,)),
            dma((uly,)),
            dma((uly,)),
            dma((4, per, shards)),
            dma((4, per, shards)),
            dma((shards,)),
            dma((shards,)),
            dma((3, uly)),
            dma((3, uly)),
            dma((3,)),
            dma((2,)),
        ],
        compiler_params=pltpu.CompilerParams(
            collective_id=0, has_side_effects=True, vmem_limit_bytes=67043328
        ),
    )(random_blocks.T, q, k, v, o, g)
    vmem = pl.BlockSpec(memory_space=pltpu.VMEM)
    return pl.pallas_call(
        write_out,
        out_shape=[jax.ShapeDtypeStruct((tok, width), jnp.bfloat16)] * 3,
        in_specs=[vmem] * 3,
        out_specs=[vmem] * 3,
        compiler_params=pltpu.CompilerParams(vmem_limit_bytes=67043328),
    )(*results)


def wide_or_fused(shards, uly, *operands):
    tok, width = operands[0].shape
    length = tok * uly
    fits = shards * length * length * 4 <= 16 * 1024 * 1024
    if fits and width == uly * HD and BLOCK % tok == 0 and length % BLOCK == 0:
        return tuple(fused_on_device(shards, uly, *operands))
    return on_device(*operands)


def solution(mesh):
    return jax.shard_map(
        functools.partial(wide_or_fused, mesh.shape["blk"], mesh.shape["uly"]),
        mesh=mesh,
        in_specs=(
            P(("blk", "uly"), None),
            P(("blk", "uly"), None),
            P(("blk", "uly"), None),
            P(("blk", "uly"), None),
            P(("blk", "uly"), None),
            P(),
        ),
        out_specs=(P(("blk", "uly"), None), P(("blk", "uly"), None), P(("blk", "uly"), None)),
        check_vma=False,
    )
```

```python
import functools
import math

import jax
import jax.numpy as jnp
from jax import lax
from jax.experimental import pallas as pl
from jax.experimental.pallas import tpu as pltpu
from jax.sharding import PartitionSpec as P

HD = 128
BLOCK = 128
RAND = 3
CAP = 2


def named_table(random_blocks, per_shard):
    block_count = random_blocks.shape[0]
    shard_count = block_count // per_shard
    entries = random_blocks.reshape(shard_count, per_shard * RAND)
    block_ids = jnp.arange(block_count, dtype=jnp.int32)
    named = jnp.any(entries[:, :, None] == block_ids[None, None, :], axis=1)
    owner = block_ids // per_shard
    named = named & (owner[None, :] != jnp.arange(shard_count, dtype=jnp.int32)[:, None])
    grouped = named.reshape(shard_count, shard_count, per_shard).astype(jnp.int32)
    rank_in = jnp.cumsum(grouped, axis=2) - grouped
    return (grouped, rank_in)


def send_slots(grouped, rank_in, cycle_rank, per_shard):
    mine = lax.dynamic_index_in_dim(grouped, cycle_rank, 1, keepdims=False)
    mine_rank = lax.dynamic_index_in_dim(rank_in, cycle_rank, 1, keepdims=False)
    slot_ids = jnp.arange(CAP, dtype=jnp.int32)
    hit = (mine[:, None, :] == 1) & (mine_rank[:, None, :] == slot_ids[None, :, None])
    positions = jnp.arange(per_shard, dtype=jnp.int32)
    select = jnp.sum(jnp.where(hit, positions[None, None, :], 0), axis=2)
    filled = jnp.any(hit, axis=2)
    return (select, filled)


def on_device(query_proj, key_proj, value_proj, attn_output, out_grad, random_blocks):
    tok_count = query_proj.shape[0]
    head_count = query_proj.shape[1] // HD
    score_scale = HD ** (-0.5)
    extent = 3 + RAND

    def to_heads(tensor):
        return tensor.reshape(tok_count, head_count, HD)

    query_rows, key_rows, value_rows, output_rows, grad_rows = (
        lax.all_to_all(to_heads(query_proj), "uly", split_axis=1, concat_axis=0, tiled=True),
        lax.all_to_all(to_heads(key_proj), "uly", split_axis=1, concat_axis=0, tiled=True),
        lax.all_to_all(to_heads(value_proj), "uly", split_axis=1, concat_axis=0, tiled=True),
        lax.all_to_all(to_heads(attn_output), "uly", split_axis=1, concat_axis=0, tiled=True),
        lax.all_to_all(to_heads(out_grad), "uly", split_axis=1, concat_axis=0, tiled=True),
    )
    row_delta = jnp.sum(
        output_rows.astype(jnp.float32) * grad_rows.astype(jnp.float32), axis=2
    ).reshape(-1)
    shard_len = query_rows.shape[0]
    per_shard = shard_len // BLOCK
    query_blocks = query_rows.reshape(per_shard, BLOCK, HD)
    key_blocks = key_rows.reshape(per_shard, BLOCK, HD)
    value_blocks = value_rows.reshape(per_shard, BLOCK, HD)
    grad_blocks = grad_rows.reshape(per_shard, BLOCK, HD)
    delta_blocks = row_delta.reshape(per_shard, BLOCK)
    cycle_size = lax.axis_size("blk")
    cycle_rank = lax.axis_index("blk")
    block_count = random_blocks.shape[0]
    grouped, rank_in = named_table(random_blocks, per_shard)
    select, filled = send_slots(grouped, rank_in, cycle_rank, per_shard)
    key_send = jnp.where(
        filled[:, :, None, None],
        jnp.take(key_blocks, select.reshape(-1), axis=0).reshape(cycle_size, CAP, BLOCK, HD),
        jnp.zeros((), jnp.bfloat16),
    )
    value_send = jnp.where(
        filled[:, :, None, None],
        jnp.take(value_blocks, select.reshape(-1), axis=0).reshape(cycle_size, CAP, BLOCK, HD),
        jnp.zeros((), jnp.bfloat16),
    )
    extra_key = jnp.broadcast_to(
        jnp.stack([key_blocks[per_shard - 1], key_blocks[0]])[None], (cycle_size, 2, BLOCK, HD)
    )
    extra_value = jnp.broadcast_to(
        jnp.stack([value_blocks[per_shard - 1], value_blocks[0]])[None], (cycle_size, 2, BLOCK, HD)
    )
    all_key, all_value = (
        lax.all_to_all(
            jnp.concatenate([key_send, extra_key], axis=1),
            "blk",
            split_axis=0,
            concat_axis=0,
            tiled=True,
        ),
        lax.all_to_all(
            jnp.concatenate([value_send, extra_value], axis=1),
            "blk",
            split_axis=0,
            concat_axis=0,
            tiled=True,
        ),
    )
    far_key = all_key[:, :CAP]
    far_value = all_value[:, :CAP]
    before_rank = jnp.maximum(cycle_rank - 1, 0)
    prev_key = lax.dynamic_index_in_dim(all_key, before_rank, 0, keepdims=False)[CAP]
    prev_value = lax.dynamic_index_in_dim(all_value, before_rank, 0, keepdims=False)[CAP]
    first_key = all_key[0, CAP + 1]
    first_value = all_value[0, CAP + 1]
    key_store = jnp.concatenate(
        [key_blocks, prev_key[None], first_key[None], far_key.reshape(cycle_size * CAP, BLOCK, HD)],
        axis=0,
    )
    value_store = jnp.concatenate(
        [
            value_blocks,
            prev_value[None],
            first_value[None],
            far_value.reshape(cycle_size * CAP, BLOCK, HD),
        ],
        axis=0,
    )
    store_size = key_store.shape[0]
    picked = lax.dynamic_slice_in_dim(random_blocks, cycle_rank * per_shard, per_shard, 0)
    own_rank = lax.dynamic_index_in_dim(rank_in, cycle_rank, 0, keepdims=False).reshape(-1)
    all_ids = jnp.arange(block_count, dtype=jnp.int32)
    slot_of = jnp.sum(
        jnp.where(picked[:, :, None] == all_ids[None, None, :], own_rank[None, None, :], 0), axis=2
    )
    owner = picked // per_shard
    random_index = jnp.where(
        owner == cycle_rank, picked - cycle_rank * per_shard, per_shard + 2 + owner * CAP + slot_of
    )
    local_ids = jnp.arange(per_shard, dtype=jnp.int32)
    global_ids = cycle_rank * per_shard + local_ids
    listed = jnp.concatenate(
        [
            global_ids[:, None],
            global_ids[:, None] - 1,
            jnp.zeros((per_shard, 1), jnp.int32),
            picked,
        ],
        axis=1,
    )
    first_index = jnp.zeros((per_shard, 1), jnp.int32) + jnp.where(
        cycle_rank == 0, 0, per_shard + 1
    ).astype(jnp.int32)
    store_index = jnp.concatenate(
        [
            local_ids[:, None],
            jnp.where(local_ids >= 1, local_ids - 1, per_shard)[:, None],
            first_index,
            random_index,
        ],
        axis=1,
    )
    order = jnp.arange(extent, dtype=jnp.int32)
    earlier = order[None, :] < order[:, None]
    repeated = jnp.any((listed[:, :, None] == listed[:, None, :]) & earlier[None, :, :], axis=2)
    usable = (listed >= 0) & jnp.logical_not(repeated)
    within = jnp.arange(BLOCK, dtype=jnp.int32)
    group = math.gcd(per_shard, max(1, 512 // BLOCK))
    group_count = per_shard // group

    def group_turn(carry, group_index):
        key_grad_store, value_grad_store = carry
        first = group_index * group
        query_grp = lax.dynamic_slice_in_dim(query_blocks, first, group, 0)
        grad_grp = lax.dynamic_slice_in_dim(grad_blocks, first, group, 0)
        delta_grp = lax.dynamic_slice_in_dim(delta_blocks, first, group, 0)
        index_grp = lax.dynamic_slice_in_dim(store_index, first, group, 0).reshape(-1)
        listed_grp = lax.dynamic_slice_in_dim(listed, first, group, 0)
        usable_grp = lax.dynamic_slice_in_dim(usable, first, group, 0)
        key_sel = jnp.take(key_store, index_grp, axis=0).reshape(group, extent * BLOCK, HD)
        value_sel = jnp.take(value_store, index_grp, axis=0).reshape(group, extent * BLOCK, HD)
        scores = (
            jnp.einsum("gqd,gkd->gqk", query_grp, key_sel, preferred_element_type=jnp.float32)
            * score_scale
        )
        query_pos = (cycle_rank * per_shard + first + jnp.arange(group, dtype=jnp.int32))[
            :, None
        ] * BLOCK + within[None, :]
        key_pos = (listed_grp[:, :, None] * BLOCK + within[None, None, :]).reshape(
            group, extent * BLOCK
        )
        allowed = jnp.repeat(usable_grp, BLOCK, axis=1)[:, None, :] & (
            key_pos[:, None, :] <= query_pos[:, :, None]
        )
        row_max = jnp.max(jnp.where(allowed, scores, -1e30), axis=2)
        total = jnp.sum(jnp.where(allowed, jnp.exp(scores - row_max[:, :, None]), 0.0), axis=2)
        log_total = row_max + jnp.log(total)
        probs = jnp.where(allowed, jnp.exp(scores - log_total[:, :, None]), 0.0)
        prob_grad = jnp.einsum(
            "gqd,gkd->gqk", grad_grp, value_sel, preferred_element_type=jnp.float32
        )
        score_grad = (probs * (prob_grad - delta_grp[:, :, None]) * score_scale).astype(
            jnp.bfloat16
        )
        query_part = jnp.einsum(
            "gqk,gkd->gqd", score_grad, key_sel, preferred_element_type=jnp.float32
        ).astype(jnp.bfloat16)
        key_part = jnp.einsum(
            "gqk,gqd->gkd", score_grad, query_grp, preferred_element_type=jnp.float32
        )
        value_part = jnp.einsum(
            "gqk,gqd->gkd", probs.astype(jnp.bfloat16), grad_grp, preferred_element_type=jnp.float32
        )
        key_grad_store = key_grad_store.at[index_grp].add(
            key_part.reshape(group * extent, BLOCK, HD)
        )
        value_grad_store = value_grad_store.at[index_grp].add(
            value_part.reshape(group * extent, BLOCK, HD)
        )
        return ((key_grad_store, value_grad_store), query_part)

    zero_store = jnp.zeros((store_size, BLOCK, HD), jnp.float32)
    (key_grad_store, value_grad_store), query_parts = lax.scan(
        group_turn, (zero_store, zero_store), jnp.arange(group_count, dtype=jnp.int32)
    )
    query_acc = query_parts.reshape(shard_len, HD)
    key_acc = key_grad_store[:per_shard]
    value_acc = value_grad_store[:per_shard]
    far_key_grad = key_grad_store[per_shard + 2 :].reshape(cycle_size, CAP, BLOCK, HD)
    far_value_grad = value_grad_store[per_shard + 2 :].reshape(cycle_size, CAP, BLOCK, HD)
    dest_ids = jnp.arange(cycle_size, dtype=jnp.int32)
    to_prev = (dest_ids == cycle_rank - 1)[:, None, None]
    to_first = (dest_ids == 0)[:, None, None]
    extra_key_grad = jnp.stack(
        [
            jnp.where(to_prev, key_grad_store[per_shard][None], 0.0),
            jnp.where(to_first, key_grad_store[per_shard + 1][None], 0.0),
        ],
        axis=1,
    )
    extra_value_grad = jnp.stack(
        [
            jnp.where(to_prev, value_grad_store[per_shard][None], 0.0),
            jnp.where(to_first, value_grad_store[per_shard + 1][None], 0.0),
        ],
        axis=1,
    )
    all_key_back, all_value_back = (
        lax.all_to_all(
            jnp.concatenate([far_key_grad, extra_key_grad], axis=1),
            "blk",
            split_axis=0,
            concat_axis=0,
            tiled=True,
        ),
        lax.all_to_all(
            jnp.concatenate([far_value_grad, extra_value_grad], axis=1),
            "blk",
            split_axis=0,
            concat_axis=0,
            tiled=True,
        ),
    )
    back_key = all_key_back[:, :CAP]
    back_value = all_value_back[:, :CAP]
    prev_back = jnp.stack(
        [jnp.sum(all_key_back[:, CAP], axis=0), jnp.sum(all_value_back[:, CAP], axis=0)]
    )
    first_back = jnp.stack(
        [jnp.sum(all_key_back[:, CAP + 1], axis=0), jnp.sum(all_value_back[:, CAP + 1], axis=0)]
    )
    key_acc = key_acc.at[per_shard - 1].add(prev_back[0]).at[0].add(first_back[0])
    value_acc = value_acc.at[per_shard - 1].add(prev_back[1]).at[0].add(first_back[1])
    back_key = jnp.where(filled[:, :, None, None], back_key, 0.0).reshape(
        cycle_size * CAP, BLOCK, HD
    )
    back_value = jnp.where(filled[:, :, None, None], back_value, 0.0).reshape(
        cycle_size * CAP, BLOCK, HD
    )
    key_acc = key_acc.at[select.reshape(-1)].add(back_key).reshape(shard_len, HD)
    value_acc = value_acc.at[select.reshape(-1)].add(back_value).reshape(shard_len, HD)
    outgoing = (
        query_acc.reshape(shard_len, 1, HD),
        key_acc.astype(jnp.bfloat16).reshape(shard_len, 1, HD),
        value_acc.astype(jnp.bfloat16).reshape(shard_len, 1, HD),
    )
    query_back, key_back, value_back = (
        lax.all_to_all(outgoing[0], "uly", split_axis=0, concat_axis=1, tiled=True),
        lax.all_to_all(outgoing[1], "uly", split_axis=0, concat_axis=1, tiled=True),
        lax.all_to_all(outgoing[2], "uly", split_axis=0, concat_axis=1, tiled=True),
    )
    return (
        query_back.reshape(tok_count, head_count * HD),
        key_back.reshape(tok_count, head_count * HD),
        value_back.reshape(tok_count, head_count * HD),
    )


NEG = -1e30
KEY, QUERY, VALUE, GRAD = 0, 1, 2, 3
ROWS_BY_COLS = (((1,), (1,)), ((), ()))
COLS_BY_COLS = (((0,), (0,)), ((), ()))


def fused_kernel(
    shards,
    uly,
    picks_hbm,
    q_ref,
    k_ref,
    v_ref,
    o_ref,
    g_ref,
    dq_ref,
    dk_ref,
    dv_ref,
    picks_ref,
    rows_in,
    held,
    delta_send,
    delta_recv,
    bias,
    stats,
    scores,
    probs_low,
    score_grads,
    acc,
    outgoing,
    zs,
    zr,
    zl,
    ds_sem,
    dr_sem,
    fs,
    fr,
    ss,
    sr,
    os_sem,
    or_sem,
    ol,
    il,
):
    tok = q_ref.shape[0]
    length = tok * uly
    per = length // BLOCK
    gp = BLOCK // tok
    blocks = per * shards
    scale = HD ** (-0.5)
    b = lax.axis_index("blk")
    u = lax.axis_index("uly")
    inputs = {KEY: k_ref, QUERY: q_ref, VALUE: v_ref, GRAD: g_ref}
    f32 = jnp.float32

    def peer(step):
        return lax.rem(u + step, uly)

    def swap_order(count, at=None):
        at = u if at is None else at
        if count & (count - 1):
            return [lax.rem(at + step, count) for step in range(1, count)]
        order = []
        for mask in range(1, count):
            other = at
            for bit in range(count.bit_length() - 1):
                if mask >> bit & 1:
                    other = other + (1 << bit) * (1 - 2 * (at // (1 << bit) % 2))
            order.append(other)
        return order

    def cols(p):
        return pl.ds(pl.multiple_of(p * HD, HD), HD)

    def rows(p):
        return pl.ds(pl.multiple_of(p * tok, tok), tok)

    def block_rows(c):
        return pl.ds(pl.multiple_of(c * BLOCK, BLOCK), BLOCK)

    def z_copy(t, p, sender):
        return pltpu.make_async_remote_copy(
            src_ref=inputs[t].at[:, cols(p)],
            dst_ref=held.at[t, b, rows(sender), :],
            send_sem=zs.at[t, p],
            recv_sem=zr.at[t, sender],
            device_id={"blk": b, "uly": p},
            device_id_type=pl.DeviceIdType.MESH,
        )

    def d_copy(p, sender):
        return pltpu.make_async_remote_copy(
            src_ref=delta_send.at[p],
            dst_ref=delta_recv.at[sender],
            send_sem=ds_sem.at[p],
            recv_sem=dr_sem.at[sender],
            device_id={"blk": b, "uly": p},
            device_id_type=pl.DeviceIdType.MESH,
        )

    def f_copy(t, c, to, sender):
        return pltpu.make_async_remote_copy(
            src_ref=held.at[t, sender, block_rows(c), :],
            dst_ref=held.at[t, sender, block_rows(c), :],
            send_sem=fs.at[t, c, to],
            recv_sem=fr.at[t, c, sender],
            device_id={"blk": to, "uly": u},
            device_id_type=pl.DeviceIdType.MESH,
        )

    def s_copy(to, sender):
        return pltpu.make_async_remote_copy(
            src_ref=stats.at[sender],
            dst_ref=stats.at[sender],
            send_sem=ss.at[to],
            recv_sem=sr.at[sender],
            device_id={"blk": to, "uly": u},
            device_id_type=pl.DeviceIdType.MESH,
        )

    results = (dq_ref, dk_ref, dv_ref)

    def o_copy(t, p, sender):
        return pltpu.make_async_remote_copy(
            src_ref=outgoing.at[t, rows(p), :],
            dst_ref=results[t].at[:, cols(sender)],
            send_sem=os_sem.at[t, p],
            recv_sem=or_sem.at[t, sender],
            device_id={"blk": b, "uly": p},
            device_id_type=pl.DeviceIdType.MESH,
        )

    def o_local(t):
        return pltpu.make_async_copy(
            outgoing.at[t, rows(u), :], results[t].at[:, cols(u)], ol.at[t]
        )

    def z_local(t):
        return pltpu.make_async_copy(inputs[t].at[:, cols(u)], held.at[t, b, rows(u), :], zl.at[t])

    fetches = (
        pltpu.make_async_copy(o_ref, rows_in.at[0], il.at[0]),
        pltpu.make_async_copy(g_ref, rows_in.at[1], il.at[1]),
        pltpu.make_async_copy(picks_hbm, picks_ref, il.at[2]),
    )
    for fetch in fetches:
        fetch.start()
    barrier = pltpu.get_barrier_semaphore()
    for step in range(1, uly):
        pl.semaphore_signal(
            barrier,
            inc=1,
            device_id={"blk": b, "uly": peer(step)},
            device_id_type=pl.DeviceIdType.MESH,
        )
    for step in range(1, shards):
        pl.semaphore_signal(
            barrier,
            inc=1,
            device_id={"blk": lax.rem(b + step, shards), "uly": u},
            device_id_type=pl.DeviceIdType.MESH,
        )
    for fetch in fetches:
        fetch.wait()
    product = rows_in[0].astype(f32) * rows_in[1].astype(f32)
    high = product.astype(jnp.bfloat16)
    low = (product - high.astype(f32)).astype(jnp.bfloat16)
    head_of = lax.broadcasted_iota(jnp.int32, (uly, uly * HD), 1) // HD
    pick_head = jnp.where(
        head_of == lax.broadcasted_iota(jnp.int32, (uly, uly * HD), 0), 1.0, 0.0
    ).astype(jnp.bfloat16)
    sums = lax.dot_general(
        pick_head, jnp.concatenate([high] * gp, axis=0), ROWS_BY_COLS, preferred_element_type=f32
    ) + lax.dot_general(
        pick_head, jnp.concatenate([low] * gp, axis=0), ROWS_BY_COLS, preferred_element_type=f32
    )
    place = lax.broadcasted_iota(jnp.int32, (uly, BLOCK), 1) // tok
    sums = jnp.where(place == lax.rem(u, gp), sums, 0.0)
    for head in range(uly):
        delta_send[head] = sums[head : head + 1]
    delta_recv[u] = delta_send[u]

    lane_block = lax.broadcasted_iota(jnp.int32, (1, length), 1) // BLOCK
    key_block = lax.broadcasted_iota(jnp.int32, (blocks, length), 0)
    for s in range(shards):
        query_block = lane_block + s * per
        hit = (key_block == query_block) | (key_block == query_block - 1) | (key_block == 0)
        for r in range(RAND):
            named = jnp.zeros((1, length), jnp.int32)
            for i in range(per):
                named = jnp.where(lane_block == i, picks_ref[r, s * per + i], named)
            hit = hit | (key_block == named)
        hit = hit & (key_block <= query_block)
        bias[s] = jnp.where(hit, 0.0, NEG)

    pl.semaphore_wait(barrier, uly - 1 + shards - 1)
    z_order = swap_order(uly)
    for pair in ((KEY, QUERY), (VALUE, GRAD)):
        for t in pair:
            z_local(t).start()
        for p in z_order:
            for t in pair:
                z_copy(t, p, u).start()
    for p in z_order:
        d_copy(p, u).start()

    own_block = u // gp

    def forward(pair):
        for t in pair:
            z_local(t).wait()
        for c in [own_block] + swap_order(per, own_block):
            for t in pair:
                for i in range(gp):
                    p = c * gp + i

                    @pl.when(p != u)
                    def _():
                        z_copy(t, p, p).wait_recv()

                for to in range(shards):
                    goes = (to > b) if t in (KEY, VALUE) else (to < b)

                    @pl.when(goes)
                    def _():
                        f_copy(t, c, to, b).start()

    def tile_scores(s_key, s_query, jb):
        keys = held[KEY, s_key, pl.ds(jb * BLOCK, BLOCK), :]
        tile = lax.dot_general(
            keys, held[QUERY, s_query], ROWS_BY_COLS, preferred_element_type=f32
        )
        return tile * scale + bias[s_query, pl.ds(s_key * per + jb, 1), :]

    forward((KEY, QUERY))

    top = jnp.full((1, length), NEG, f32)
    for jb in range(per):
        tile = tile_scores(b, b, jb)
        key_at = lax.broadcasted_iota(jnp.int32, (BLOCK, length), 0) + jb * BLOCK
        query_at = lax.broadcasted_iota(jnp.int32, (BLOCK, length), 1)
        tile = jnp.where(key_at <= query_at, tile, NEG)
        scores[b, pl.ds(jb * BLOCK, BLOCK), :] = tile
        top = jnp.maximum(top, jnp.max(tile, axis=0, keepdims=True))

    forward((VALUE, GRAD))

    def far_scores(s, top):
        for jb in range(per):
            f_copy(KEY, jb, b, s).wait_recv()
            tile = tile_scores(s, b, jb)
            scores[s, pl.ds(jb * BLOCK, BLOCK), :] = tile
            top = jnp.maximum(top, jnp.max(tile, axis=0, keepdims=True))
        return top

    top = lax.fori_loop(0, b, far_scores, top)

    def add_exp(s, total):
        for jb in range(per):
            tile = jnp.exp(scores[s, pl.ds(jb * BLOCK, BLOCK), :] - top)
            total = total + jnp.sum(tile, axis=0, keepdims=True)
        return total

    total = lax.fori_loop(0, b + 1, add_exp, jnp.zeros((1, length), f32))
    log_total = top + jnp.log(total)
    for step in range(1, uly):
        d_copy(peer(step), peer(step)).wait_recv()
    pieces = []
    for c in range(per):
        piece = delta_recv[c * gp]
        for i in range(1, gp):
            piece = piece + delta_recv[c * gp + i]
        pieces.append(piece)
    delta = jnp.concatenate(pieces, axis=1)
    stats[b, 0:1, :] = log_total
    stats[b, 1:2, :] = delta
    for to in range(shards):

        @pl.when(to < b)
        def _():
            s_copy(to, b).start()

    def tile_grads(tile, s_key, s_query, jb, log_row, delta_row):
        probs = jnp.exp(tile - log_row)
        values = held[VALUE, s_key, pl.ds(jb * BLOCK, BLOCK), :]
        prob_grad = lax.dot_general(
            values, held[GRAD, s_query], ROWS_BY_COLS, preferred_element_type=f32
        )
        grads = (probs * (prob_grad - delta_row) * scale).astype(jnp.bfloat16)
        return probs.astype(jnp.bfloat16), grads

    for jb in range(per):
        probs, grads = tile_grads(
            scores[b, pl.ds(jb * BLOCK, BLOCK), :], b, b, jb, log_total, delta
        )
        probs_low[pl.ds(jb * BLOCK, BLOCK), :] = probs
        score_grads[pl.ds(jb * BLOCK, BLOCK), :] = grads
    acc[0] = lax.dot_general(
        score_grads[...], held[KEY, b], COLS_BY_COLS, preferred_element_type=f32
    )
    acc[1] = jnp.dot(score_grads[...], held[QUERY, b], preferred_element_type=f32)
    acc[2] = jnp.dot(probs_low[...], held[GRAD, b], preferred_element_type=f32)

    def send_result(t):
        outgoing[t] = acc[t].astype(jnp.bfloat16)
        for p in z_order:
            o_copy(t, p, u).start()
        o_local(t).start()

    @pl.when(b == shards - 1)
    def _():
        send_result(1)
        send_result(2)

    def far_keys(s, carry):
        for jb in range(per):
            f_copy(VALUE, jb, b, s).wait_recv()
            _, grads = tile_grads(
                scores[s, pl.ds(jb * BLOCK, BLOCK), :], s, b, jb, log_total, delta
            )
            score_grads[pl.ds(jb * BLOCK, BLOCK), :] = grads
        acc[0] += lax.dot_general(
            score_grads[...], held[KEY, s], COLS_BY_COLS, preferred_element_type=f32
        )
        return carry

    lax.fori_loop(0, b, far_keys, 0)

    send_result(0)

    def far_queries(s, carry):
        for c in range(per):
            f_copy(QUERY, c, b, s).wait_recv()
            f_copy(GRAD, c, b, s).wait_recv()
        s_copy(b, s).wait_recv()
        log_row = stats[s, 0:1, :]
        delta_row = stats[s, 1:2, :]
        for jb in range(per):
            probs, grads = tile_grads(tile_scores(b, s, jb), b, s, jb, log_row, delta_row)
            probs_low[pl.ds(jb * BLOCK, BLOCK), :] = probs
            score_grads[pl.ds(jb * BLOCK, BLOCK), :] = grads
        acc[1] += jnp.dot(score_grads[...], held[QUERY, s], preferred_element_type=f32)
        acc[2] += jnp.dot(probs_low[...], held[GRAD, s], preferred_element_type=f32)
        return carry

    @pl.when(b < shards - 1)
    def _():
        lax.fori_loop(b + 1, shards, far_queries, 0)
        send_result(1)
        send_result(2)


    for step in range(1, uly):
        p = peer(step)
        d_copy(p, u).wait_send()
        for t in (KEY, QUERY, VALUE, GRAD):
            z_copy(t, p, u).wait_send()
    for to in range(shards):

        @pl.when(to > b)
        def _():
            for c in range(per):
                f_copy(KEY, c, to, b).wait_send()
                f_copy(VALUE, c, to, b).wait_send()

        @pl.when(to < b)
        def _():
            for c in range(per):
                f_copy(QUERY, c, to, b).wait_send()
                f_copy(GRAD, c, to, b).wait_send()
            s_copy(to, b).wait_send()

    for t in range(3):
        o_local(t).wait()
        for step in range(1, uly):
            p = peer(step)
            o_copy(t, p, p).wait_recv()
            o_copy(t, p, u).wait_send()


def write_out(a_ref, b_ref, c_ref, a_out, b_out, c_out):
    a_out[...] = a_ref[...]
    b_out[...] = b_ref[...]
    c_out[...] = c_ref[...]


def fused_on_device(shards, uly, q, k, v, o, g, random_blocks):
    tok, width = q.shape
    length = tok * uly
    per = length // BLOCK
    dma = pltpu.SemaphoreType.DMA
    hbm = pl.BlockSpec(memory_space=pltpu.HBM)
    results = pl.pallas_call(
        functools.partial(fused_kernel, shards, uly),
        out_shape=[jax.ShapeDtypeStruct((tok, width), jnp.bfloat16)] * 3,
        in_specs=[hbm] * 6,
        out_specs=[hbm] * 3,
        scratch_shapes=[
            pltpu.SMEM(random_blocks.shape[::-1], jnp.int32),
            pltpu.VMEM((2, tok, width), jnp.bfloat16),
            pltpu.VMEM((4, shards, length, HD), jnp.bfloat16),
            pltpu.VMEM((uly, 1, BLOCK), jnp.float32),
            pltpu.VMEM((uly, 1, BLOCK), jnp.float32),
            pltpu.VMEM((shards, shards * per, length), jnp.float32),
            pltpu.VMEM((shards, 2, length), jnp.float32),
            pltpu.VMEM((shards, length, length), jnp.float32),
            pltpu.VMEM((length, length), jnp.bfloat16),
            pltpu.VMEM((length, length), jnp.bfloat16),
            pltpu.VMEM((3, length, HD), jnp.float32),
            pltpu.VMEM((3, length, HD), jnp.bfloat16),
            dma((4, uly)),
            dma((4, uly)),
            dma((4,)),
            dma((uly,)),
            dma((uly,)),
            dma((4, per, shards)),
            dma((4, per, shards)),
            dma((shards,)),
            dma((shards,)),
            dma((3, uly)),
            dma((3, uly)),
            dma((3,)),
            dma((3,)),
        ],
        compiler_params=pltpu.CompilerParams(
            collective_id=0, has_side_effects=True, vmem_limit_bytes=67043328
        ),
    )(random_blocks.T, q, k, v, o, g)
    vmem = pl.BlockSpec(memory_space=pltpu.VMEM)
    return pl.pallas_call(
        write_out,
        out_shape=[jax.ShapeDtypeStruct((tok, width), jnp.bfloat16)] * 3,
        in_specs=[vmem] * 3,
        out_specs=[vmem] * 3,
        compiler_params=pltpu.CompilerParams(vmem_limit_bytes=67043328),
    )(*results)


def wide_or_fused(shards, uly, *operands):
    tok, width = operands[0].shape
    length = tok * uly
    fits = shards * length * length * 4 <= 16 * 1024 * 1024
    if fits and width == uly * HD and BLOCK % tok == 0 and length % BLOCK == 0:
        return tuple(fused_on_device(shards, uly, *operands))
    return on_device(*operands)


def solution(mesh):
    return jax.shard_map(
        functools.partial(wide_or_fused, mesh.shape["blk"], mesh.shape["uly"]),
        mesh=mesh,
        in_specs=(
            P(("blk", "uly"), None),
            P(("blk", "uly"), None),
            P(("blk", "uly"), None),
            P(("blk", "uly"), None),
            P(("blk", "uly"), None),
            P(),
        ),
        out_specs=(P(("blk", "uly"), None), P(("blk", "uly"), None), P(("blk", "uly"), None)),
        check_vma=False,
    )
```

```python
import functools
import math

import jax
import jax.numpy as jnp
from jax import lax
from jax.experimental import pallas as pl
from jax.experimental.pallas import tpu as pltpu
from jax.sharding import PartitionSpec as P

HD = 128
BLOCK = 128
RAND = 3
CAP = 2


def named_table(random_blocks, per_shard):
    block_count = random_blocks.shape[0]
    shard_count = block_count // per_shard
    entries = random_blocks.reshape(shard_count, per_shard * RAND)
    block_ids = jnp.arange(block_count, dtype=jnp.int32)
    named = jnp.any(entries[:, :, None] == block_ids[None, None, :], axis=1)
    owner = block_ids // per_shard
    named = named & (owner[None, :] != jnp.arange(shard_count, dtype=jnp.int32)[:, None])
    grouped = named.reshape(shard_count, shard_count, per_shard).astype(jnp.int32)
    rank_in = jnp.cumsum(grouped, axis=2) - grouped
    return (grouped, rank_in)


def send_slots(grouped, rank_in, cycle_rank, per_shard):
    mine = lax.dynamic_index_in_dim(grouped, cycle_rank, 1, keepdims=False)
    mine_rank = lax.dynamic_index_in_dim(rank_in, cycle_rank, 1, keepdims=False)
    slot_ids = jnp.arange(CAP, dtype=jnp.int32)
    hit = (mine[:, None, :] == 1) & (mine_rank[:, None, :] == slot_ids[None, :, None])
    positions = jnp.arange(per_shard, dtype=jnp.int32)
    select = jnp.sum(jnp.where(hit, positions[None, None, :], 0), axis=2)
    filled = jnp.any(hit, axis=2)
    return (select, filled)


def on_device(query_proj, key_proj, value_proj, attn_output, out_grad, random_blocks):
    tok_count = query_proj.shape[0]
    head_count = query_proj.shape[1] // HD
    score_scale = HD ** (-0.5)
    extent = 3 + RAND

    def to_heads(tensor):
        return tensor.reshape(tok_count, head_count, HD)

    query_rows, key_rows, value_rows, output_rows, grad_rows = (
        lax.all_to_all(to_heads(query_proj), "uly", split_axis=1, concat_axis=0, tiled=True),
        lax.all_to_all(to_heads(key_proj), "uly", split_axis=1, concat_axis=0, tiled=True),
        lax.all_to_all(to_heads(value_proj), "uly", split_axis=1, concat_axis=0, tiled=True),
        lax.all_to_all(to_heads(attn_output), "uly", split_axis=1, concat_axis=0, tiled=True),
        lax.all_to_all(to_heads(out_grad), "uly", split_axis=1, concat_axis=0, tiled=True),
    )
    row_delta = jnp.sum(
        output_rows.astype(jnp.float32) * grad_rows.astype(jnp.float32), axis=2
    ).reshape(-1)
    shard_len = query_rows.shape[0]
    per_shard = shard_len // BLOCK
    query_blocks = query_rows.reshape(per_shard, BLOCK, HD)
    key_blocks = key_rows.reshape(per_shard, BLOCK, HD)
    value_blocks = value_rows.reshape(per_shard, BLOCK, HD)
    grad_blocks = grad_rows.reshape(per_shard, BLOCK, HD)
    delta_blocks = row_delta.reshape(per_shard, BLOCK)
    cycle_size = lax.axis_size("blk")
    cycle_rank = lax.axis_index("blk")
    block_count = random_blocks.shape[0]
    grouped, rank_in = named_table(random_blocks, per_shard)
    select, filled = send_slots(grouped, rank_in, cycle_rank, per_shard)
    key_send = jnp.where(
        filled[:, :, None, None],
        jnp.take(key_blocks, select.reshape(-1), axis=0).reshape(cycle_size, CAP, BLOCK, HD),
        jnp.zeros((), jnp.bfloat16),
    )
    value_send = jnp.where(
        filled[:, :, None, None],
        jnp.take(value_blocks, select.reshape(-1), axis=0).reshape(cycle_size, CAP, BLOCK, HD),
        jnp.zeros((), jnp.bfloat16),
    )
    extra_key = jnp.broadcast_to(
        jnp.stack([key_blocks[per_shard - 1], key_blocks[0]])[None], (cycle_size, 2, BLOCK, HD)
    )
    extra_value = jnp.broadcast_to(
        jnp.stack([value_blocks[per_shard - 1], value_blocks[0]])[None], (cycle_size, 2, BLOCK, HD)
    )
    all_key, all_value = (
        lax.all_to_all(
            jnp.concatenate([key_send, extra_key], axis=1),
            "blk",
            split_axis=0,
            concat_axis=0,
            tiled=True,
        ),
        lax.all_to_all(
            jnp.concatenate([value_send, extra_value], axis=1),
            "blk",
            split_axis=0,
            concat_axis=0,
            tiled=True,
        ),
    )
    far_key = all_key[:, :CAP]
    far_value = all_value[:, :CAP]
    before_rank = jnp.maximum(cycle_rank - 1, 0)
    prev_key = lax.dynamic_index_in_dim(all_key, before_rank, 0, keepdims=False)[CAP]
    prev_value = lax.dynamic_index_in_dim(all_value, before_rank, 0, keepdims=False)[CAP]
    first_key = all_key[0, CAP + 1]
    first_value = all_value[0, CAP + 1]
    key_store = jnp.concatenate(
        [key_blocks, prev_key[None], first_key[None], far_key.reshape(cycle_size * CAP, BLOCK, HD)],
        axis=0,
    )
    value_store = jnp.concatenate(
        [
            value_blocks,
            prev_value[None],
            first_value[None],
            far_value.reshape(cycle_size * CAP, BLOCK, HD),
        ],
        axis=0,
    )
    store_size = key_store.shape[0]
    picked = lax.dynamic_slice_in_dim(random_blocks, cycle_rank * per_shard, per_shard, 0)
    own_rank = lax.dynamic_index_in_dim(rank_in, cycle_rank, 0, keepdims=False).reshape(-1)
    all_ids = jnp.arange(block_count, dtype=jnp.int32)
    slot_of = jnp.sum(
        jnp.where(picked[:, :, None] == all_ids[None, None, :], own_rank[None, None, :], 0), axis=2
    )
    owner = picked // per_shard
    random_index = jnp.where(
        owner == cycle_rank, picked - cycle_rank * per_shard, per_shard + 2 + owner * CAP + slot_of
    )
    local_ids = jnp.arange(per_shard, dtype=jnp.int32)
    global_ids = cycle_rank * per_shard + local_ids
    listed = jnp.concatenate(
        [
            global_ids[:, None],
            global_ids[:, None] - 1,
            jnp.zeros((per_shard, 1), jnp.int32),
            picked,
        ],
        axis=1,
    )
    first_index = jnp.zeros((per_shard, 1), jnp.int32) + jnp.where(
        cycle_rank == 0, 0, per_shard + 1
    ).astype(jnp.int32)
    store_index = jnp.concatenate(
        [
            local_ids[:, None],
            jnp.where(local_ids >= 1, local_ids - 1, per_shard)[:, None],
            first_index,
            random_index,
        ],
        axis=1,
    )
    order = jnp.arange(extent, dtype=jnp.int32)
    earlier = order[None, :] < order[:, None]
    repeated = jnp.any((listed[:, :, None] == listed[:, None, :]) & earlier[None, :, :], axis=2)
    usable = (listed >= 0) & jnp.logical_not(repeated)
    within = jnp.arange(BLOCK, dtype=jnp.int32)
    group = math.gcd(per_shard, max(1, 512 // BLOCK))
    group_count = per_shard // group

    def group_turn(carry, group_index):
        key_grad_store, value_grad_store = carry
        first = group_index * group
        query_grp = lax.dynamic_slice_in_dim(query_blocks, first, group, 0)
        grad_grp = lax.dynamic_slice_in_dim(grad_blocks, first, group, 0)
        delta_grp = lax.dynamic_slice_in_dim(delta_blocks, first, group, 0)
        index_grp = lax.dynamic_slice_in_dim(store_index, first, group, 0).reshape(-1)
        listed_grp = lax.dynamic_slice_in_dim(listed, first, group, 0)
        usable_grp = lax.dynamic_slice_in_dim(usable, first, group, 0)
        key_sel = jnp.take(key_store, index_grp, axis=0).reshape(group, extent * BLOCK, HD)
        value_sel = jnp.take(value_store, index_grp, axis=0).reshape(group, extent * BLOCK, HD)
        scores = (
            jnp.einsum("gqd,gkd->gqk", query_grp, key_sel, preferred_element_type=jnp.float32)
            * score_scale
        )
        query_pos = (cycle_rank * per_shard + first + jnp.arange(group, dtype=jnp.int32))[
            :, None
        ] * BLOCK + within[None, :]
        key_pos = (listed_grp[:, :, None] * BLOCK + within[None, None, :]).reshape(
            group, extent * BLOCK
        )
        allowed = jnp.repeat(usable_grp, BLOCK, axis=1)[:, None, :] & (
            key_pos[:, None, :] <= query_pos[:, :, None]
        )
        row_max = jnp.max(jnp.where(allowed, scores, -1e30), axis=2)
        total = jnp.sum(jnp.where(allowed, jnp.exp(scores - row_max[:, :, None]), 0.0), axis=2)
        log_total = row_max + jnp.log(total)
        probs = jnp.where(allowed, jnp.exp(scores - log_total[:, :, None]), 0.0)
        prob_grad = jnp.einsum(
            "gqd,gkd->gqk", grad_grp, value_sel, preferred_element_type=jnp.float32
        )
        score_grad = (probs * (prob_grad - delta_grp[:, :, None]) * score_scale).astype(
            jnp.bfloat16
        )
        query_part = jnp.einsum(
            "gqk,gkd->gqd", score_grad, key_sel, preferred_element_type=jnp.float32
        ).astype(jnp.bfloat16)
        key_part = jnp.einsum(
            "gqk,gqd->gkd", score_grad, query_grp, preferred_element_type=jnp.float32
        )
        value_part = jnp.einsum(
            "gqk,gqd->gkd", probs.astype(jnp.bfloat16), grad_grp, preferred_element_type=jnp.float32
        )
        key_grad_store = key_grad_store.at[index_grp].add(
            key_part.reshape(group * extent, BLOCK, HD)
        )
        value_grad_store = value_grad_store.at[index_grp].add(
            value_part.reshape(group * extent, BLOCK, HD)
        )
        return ((key_grad_store, value_grad_store), query_part)

    zero_store = jnp.zeros((store_size, BLOCK, HD), jnp.float32)
    (key_grad_store, value_grad_store), query_parts = lax.scan(
        group_turn, (zero_store, zero_store), jnp.arange(group_count, dtype=jnp.int32)
    )
    query_acc = query_parts.reshape(shard_len, HD)
    key_acc = key_grad_store[:per_shard]
    value_acc = value_grad_store[:per_shard]
    far_key_grad = key_grad_store[per_shard + 2 :].reshape(cycle_size, CAP, BLOCK, HD)
    far_value_grad = value_grad_store[per_shard + 2 :].reshape(cycle_size, CAP, BLOCK, HD)
    dest_ids = jnp.arange(cycle_size, dtype=jnp.int32)
    to_prev = (dest_ids == cycle_rank - 1)[:, None, None]
    to_first = (dest_ids == 0)[:, None, None]
    extra_key_grad = jnp.stack(
        [
            jnp.where(to_prev, key_grad_store[per_shard][None], 0.0),
            jnp.where(to_first, key_grad_store[per_shard + 1][None], 0.0),
        ],
        axis=1,
    )
    extra_value_grad = jnp.stack(
        [
            jnp.where(to_prev, value_grad_store[per_shard][None], 0.0),
            jnp.where(to_first, value_grad_store[per_shard + 1][None], 0.0),
        ],
        axis=1,
    )
    all_key_back, all_value_back = (
        lax.all_to_all(
            jnp.concatenate([far_key_grad, extra_key_grad], axis=1),
            "blk",
            split_axis=0,
            concat_axis=0,
            tiled=True,
        ),
        lax.all_to_all(
            jnp.concatenate([far_value_grad, extra_value_grad], axis=1),
            "blk",
            split_axis=0,
            concat_axis=0,
            tiled=True,
        ),
    )
    back_key = all_key_back[:, :CAP]
    back_value = all_value_back[:, :CAP]
    prev_back = jnp.stack(
        [jnp.sum(all_key_back[:, CAP], axis=0), jnp.sum(all_value_back[:, CAP], axis=0)]
    )
    first_back = jnp.stack(
        [jnp.sum(all_key_back[:, CAP + 1], axis=0), jnp.sum(all_value_back[:, CAP + 1], axis=0)]
    )
    key_acc = key_acc.at[per_shard - 1].add(prev_back[0]).at[0].add(first_back[0])
    value_acc = value_acc.at[per_shard - 1].add(prev_back[1]).at[0].add(first_back[1])
    back_key = jnp.where(filled[:, :, None, None], back_key, 0.0).reshape(
        cycle_size * CAP, BLOCK, HD
    )
    back_value = jnp.where(filled[:, :, None, None], back_value, 0.0).reshape(
        cycle_size * CAP, BLOCK, HD
    )
    key_acc = key_acc.at[select.reshape(-1)].add(back_key).reshape(shard_len, HD)
    value_acc = value_acc.at[select.reshape(-1)].add(back_value).reshape(shard_len, HD)
    outgoing = (
        query_acc.reshape(shard_len, 1, HD),
        key_acc.astype(jnp.bfloat16).reshape(shard_len, 1, HD),
        value_acc.astype(jnp.bfloat16).reshape(shard_len, 1, HD),
    )
    query_back, key_back, value_back = (
        lax.all_to_all(outgoing[0], "uly", split_axis=0, concat_axis=1, tiled=True),
        lax.all_to_all(outgoing[1], "uly", split_axis=0, concat_axis=1, tiled=True),
        lax.all_to_all(outgoing[2], "uly", split_axis=0, concat_axis=1, tiled=True),
    )
    return (
        query_back.reshape(tok_count, head_count * HD),
        key_back.reshape(tok_count, head_count * HD),
        value_back.reshape(tok_count, head_count * HD),
    )


NEG = -1e30
KEY, QUERY, VALUE, GRAD = 0, 1, 2, 3
ROWS_BY_COLS = (((1,), (1,)), ((), ()))
COLS_BY_COLS = (((0,), (0,)), ((), ()))


def fused_kernel(
    shards,
    uly,
    picks_hbm,
    q_ref,
    k_ref,
    v_ref,
    o_ref,
    g_ref,
    dq_ref,
    dk_ref,
    dv_ref,
    picks_ref,
    rows_in,
    held,
    delta_send,
    delta_recv,
    bias,
    stats,
    scores,
    probs_low,
    score_grads,
    acc,
    outgoing,
    zs,
    zr,
    zl,
    ds_sem,
    dr_sem,
    fs,
    fr,
    ss,
    sr,
    os_sem,
    or_sem,
    ol,
    il,
):
    tok = q_ref.shape[0]
    length = tok * uly
    per = length // BLOCK
    gp = BLOCK // tok
    blocks = per * shards
    scale = HD ** (-0.5)
    b = lax.axis_index("blk")
    u = lax.axis_index("uly")
    inputs = {KEY: k_ref, QUERY: q_ref, VALUE: v_ref, GRAD: g_ref}
    f32 = jnp.float32

    def peer(step):
        return lax.rem(u + step, uly)

    def swap_order(count, at=None):
        at = u if at is None else at
        if count & (count - 1):
            return [lax.rem(at + step, count) for step in range(1, count)]
        order = []
        for mask in range(1, count):
            other = at
            for bit in range(count.bit_length() - 1):
                if mask >> bit & 1:
                    other = other + (1 << bit) * (1 - 2 * (at // (1 << bit) % 2))
            order.append(other)
        return order

    def cols(p):
        return pl.ds(pl.multiple_of(p * HD, HD), HD)

    def rows(p):
        return pl.ds(pl.multiple_of(p * tok, tok), tok)

    def block_rows(c):
        return pl.ds(pl.multiple_of(c * BLOCK, BLOCK), BLOCK)

    def z_copy(t, p, sender):
        return pltpu.make_async_remote_copy(
            src_ref=inputs[t].at[:, cols(p)],
            dst_ref=held.at[t, b, rows(sender), :],
            send_sem=zs.at[t, p],
            recv_sem=zr.at[t, sender],
            device_id={"blk": b, "uly": p},
            device_id_type=pl.DeviceIdType.MESH,
        )

    def d_copy(p, sender):
        return pltpu.make_async_remote_copy(
            src_ref=delta_send.at[p],
            dst_ref=delta_recv.at[sender],
            send_sem=ds_sem.at[p],
            recv_sem=dr_sem.at[sender],
            device_id={"blk": b, "uly": p},
            device_id_type=pl.DeviceIdType.MESH,
        )

    def f_copy(t, c, to, sender):
        return pltpu.make_async_remote_copy(
            src_ref=held.at[t, sender, block_rows(c), :],
            dst_ref=held.at[t, sender, block_rows(c), :],
            send_sem=fs.at[t, c, to],
            recv_sem=fr.at[t, c, sender],
            device_id={"blk": to, "uly": u},
            device_id_type=pl.DeviceIdType.MESH,
        )

    def s_copy(to, sender):
        return pltpu.make_async_remote_copy(
            src_ref=stats.at[sender],
            dst_ref=stats.at[sender],
            send_sem=ss.at[to],
            recv_sem=sr.at[sender],
            device_id={"blk": to, "uly": u},
            device_id_type=pl.DeviceIdType.MESH,
        )

    results = (dq_ref, dk_ref, dv_ref)

    def o_copy(t, p, sender):
        return pltpu.make_async_remote_copy(
            src_ref=outgoing.at[t, rows(p), :],
            dst_ref=results[t].at[:, cols(sender)],
            send_sem=os_sem.at[t, p],
            recv_sem=or_sem.at[t, sender],
            device_id={"blk": b, "uly": p},
            device_id_type=pl.DeviceIdType.MESH,
        )

    def o_local(t):
        return pltpu.make_async_copy(
            outgoing.at[t, rows(u), :], results[t].at[:, cols(u)], ol.at[t]
        )

    def z_local(t):
        return pltpu.make_async_copy(inputs[t].at[:, cols(u)], held.at[t, b, rows(u), :], zl.at[t])

    fetches = (
        pltpu.make_async_copy(o_ref, rows_in.at[0], il.at[0]),
        pltpu.make_async_copy(g_ref, rows_in.at[1], il.at[1]),
        pltpu.make_async_copy(picks_hbm, picks_ref, il.at[2]),
    )
    for fetch in fetches:
        fetch.start()
    barrier = pltpu.get_barrier_semaphore()
    for step in range(1, uly):
        pl.semaphore_signal(
            barrier,
            inc=1,
            device_id={"blk": b, "uly": peer(step)},
            device_id_type=pl.DeviceIdType.MESH,
        )
    for step in range(1, shards):
        pl.semaphore_signal(
            barrier,
            inc=1,
            device_id={"blk": lax.rem(b + step, shards), "uly": u},
            device_id_type=pl.DeviceIdType.MESH,
        )
    for fetch in fetches:
        fetch.wait()
    product = rows_in[0].astype(f32) * rows_in[1].astype(f32)
    high = product.astype(jnp.bfloat16)
    low = (product - high.astype(f32)).astype(jnp.bfloat16)
    head_of = lax.broadcasted_iota(jnp.int32, (uly, uly * HD), 1) // HD
    pick_head = jnp.where(
        head_of == lax.broadcasted_iota(jnp.int32, (uly, uly * HD), 0), 1.0, 0.0
    ).astype(jnp.bfloat16)
    sums = lax.dot_general(
        pick_head, jnp.concatenate([high] * gp, axis=0), ROWS_BY_COLS, preferred_element_type=f32
    ) + lax.dot_general(
        pick_head, jnp.concatenate([low] * gp, axis=0), ROWS_BY_COLS, preferred_element_type=f32
    )
    place = lax.broadcasted_iota(jnp.int32, (uly, BLOCK), 1) // tok
    sums = jnp.where(place == lax.rem(u, gp), sums, 0.0)
    for head in range(uly):
        delta_send[head] = sums[head : head + 1]
    delta_recv[u] = delta_send[u]

    lane_block = lax.broadcasted_iota(jnp.int32, (1, length), 1) // BLOCK
    key_block = lax.broadcasted_iota(jnp.int32, (blocks, length), 0)
    for s in range(shards):
        query_block = lane_block + s * per
        hit = (key_block == query_block) | (key_block == query_block - 1) | (key_block == 0)
        for r in range(RAND):
            named = jnp.zeros((1, length), jnp.int32)
            for i in range(per):
                named = jnp.where(lane_block == i, picks_ref[r, s * per + i], named)
            hit = hit | (key_block == named)
        hit = hit & (key_block <= query_block)
        bias[s] = jnp.where(hit, 0.0, NEG)

    pl.semaphore_wait(barrier, uly - 1 + shards - 1)
    z_order = swap_order(uly)
    for pair in ((KEY, QUERY), (VALUE, GRAD)):
        for t in pair:
            z_local(t).start()
        for p in z_order:
            for t in pair:
                z_copy(t, p, u).start()
    for p in z_order:
        d_copy(p, u).start()

    own_block = u // gp

    def forward(pair):
        for t in pair:
            z_local(t).wait()
        for c in [own_block] + swap_order(per, own_block):
            for t in pair:
                for i in range(gp):
                    p = c * gp + i

                    @pl.when(p != u)
                    def _():
                        z_copy(t, p, p).wait_recv()

                for to in range(shards):
                    goes = (to > b) if t in (KEY, VALUE) else (to < b)

                    @pl.when(goes)
                    def _():
                        f_copy(t, c, to, b).start()

    def tile_scores(s_key, s_query, jb):
        keys = held[KEY, s_key, pl.ds(jb * BLOCK, BLOCK), :]
        tile = lax.dot_general(
            keys, held[QUERY, s_query], ROWS_BY_COLS, preferred_element_type=f32
        )
        return tile * scale + bias[s_query, pl.ds(s_key * per + jb, 1), :]

    forward((KEY, QUERY))

    top = jnp.full((1, length), NEG, f32)
    for jb in range(per):
        tile = tile_scores(b, b, jb)
        key_at = lax.broadcasted_iota(jnp.int32, (BLOCK, length), 0) + jb * BLOCK
        query_at = lax.broadcasted_iota(jnp.int32, (BLOCK, length), 1)
        tile = jnp.where(key_at <= query_at, tile, NEG)
        scores[b, pl.ds(jb * BLOCK, BLOCK), :] = tile
        top = jnp.maximum(top, jnp.max(tile, axis=0, keepdims=True))

    forward((VALUE, GRAD))

    def far_scores(s, top):
        for jb in range(per):
            f_copy(KEY, jb, b, s).wait_recv()
            tile = tile_scores(s, b, jb)
            scores[s, pl.ds(jb * BLOCK, BLOCK), :] = tile
            top = jnp.maximum(top, jnp.max(tile, axis=0, keepdims=True))
        return top

    top = lax.fori_loop(0, b, far_scores, top)

    def add_exp(s, total):
        for jb in range(per):
            tile = jnp.exp(scores[s, pl.ds(jb * BLOCK, BLOCK), :] - top)
            total = total + jnp.sum(tile, axis=0, keepdims=True)
        return total

    total = lax.fori_loop(0, b + 1, add_exp, jnp.zeros((1, length), f32))
    log_total = top + jnp.log(total)
    for step in range(1, uly):
        d_copy(peer(step), peer(step)).wait_recv()
    pieces = []
    for c in range(per):
        piece = delta_recv[c * gp]
        for i in range(1, gp):
            piece = piece + delta_recv[c * gp + i]
        pieces.append(piece)
    delta = jnp.concatenate(pieces, axis=1)
    stats[b, 0:1, :] = log_total
    stats[b, 1:2, :] = delta
    for to in range(shards):

        @pl.when(to < b)
        def _():
            s_copy(to, b).start()

    def tile_grads(tile, s_key, s_query, jb, log_row, delta_row):
        probs = jnp.exp(tile - log_row)
        values = held[VALUE, s_key, pl.ds(jb * BLOCK, BLOCK), :]
        prob_grad = lax.dot_general(
            values, held[GRAD, s_query], ROWS_BY_COLS, preferred_element_type=f32
        )
        grads = (probs * (prob_grad - delta_row) * scale).astype(jnp.bfloat16)
        return probs.astype(jnp.bfloat16), grads

    for jb in range(per):
        probs, grads = tile_grads(
            scores[b, pl.ds(jb * BLOCK, BLOCK), :], b, b, jb, log_total, delta
        )
        probs_low[pl.ds(jb * BLOCK, BLOCK), :] = probs
        score_grads[pl.ds(jb * BLOCK, BLOCK), :] = grads
    acc[0] = lax.dot_general(
        score_grads[...], held[KEY, b], COLS_BY_COLS, preferred_element_type=f32
    )
    acc[1] = jnp.dot(score_grads[...], held[QUERY, b], preferred_element_type=f32)
    acc[2] = jnp.dot(probs_low[...], held[GRAD, b], preferred_element_type=f32)

    def send_result(t):
        outgoing[t] = acc[t].astype(jnp.bfloat16)
        for p in z_order:
            o_copy(t, p, u).start()
        o_local(t).start()

    @pl.when(b == shards - 1)
    def _():
        send_result(1)
        send_result(2)

    def far_keys(s, carry):
        for jb in range(per):
            f_copy(VALUE, jb, b, s).wait_recv()
            _, grads = tile_grads(
                scores[s, pl.ds(jb * BLOCK, BLOCK), :], s, b, jb, log_total, delta
            )
            score_grads[pl.ds(jb * BLOCK, BLOCK), :] = grads
        acc[0] += lax.dot_general(
            score_grads[...], held[KEY, s], COLS_BY_COLS, preferred_element_type=f32
        )
        return carry

    lax.fori_loop(0, b, far_keys, 0)

    send_result(0)

    def far_queries(s, carry):
        for c in range(per):
            f_copy(QUERY, c, b, s).wait_recv()
            f_copy(GRAD, c, b, s).wait_recv()
        s_copy(b, s).wait_recv()
        log_row = stats[s, 0:1, :]
        delta_row = stats[s, 1:2, :]
        for jb in range(per):
            probs, grads = tile_grads(tile_scores(b, s, jb), b, s, jb, log_row, delta_row)
            probs_low[pl.ds(jb * BLOCK, BLOCK), :] = probs
            score_grads[pl.ds(jb * BLOCK, BLOCK), :] = grads
        acc[1] += jnp.dot(score_grads[...], held[QUERY, s], preferred_element_type=f32)
        acc[2] += jnp.dot(probs_low[...], held[GRAD, s], preferred_element_type=f32)
        return carry

    @pl.when(b < shards - 1)
    def _():
        lax.fori_loop(b + 1, shards, far_queries, 0)
        send_result(1)
        send_result(2)


    for step in range(1, uly):
        p = peer(step)
        d_copy(p, u).wait_send()
        for t in (KEY, QUERY, VALUE, GRAD):
            z_copy(t, p, u).wait_send()
    for to in range(shards):

        @pl.when(to > b)
        def _():
            for c in range(per):
                f_copy(KEY, c, to, b).wait_send()
                f_copy(VALUE, c, to, b).wait_send()

        @pl.when(to < b)
        def _():
            for c in range(per):
                f_copy(QUERY, c, to, b).wait_send()
                f_copy(GRAD, c, to, b).wait_send()
            s_copy(to, b).wait_send()

    for t in range(3):
        o_local(t).wait()
        for step in range(1, uly):
            p = peer(step)
            o_copy(t, p, p).wait_recv()
            o_copy(t, p, u).wait_send()


def write_out(a_ref, b_ref, c_ref, a_out, b_out, c_out, held, arrived, done):
    pairs = ((a_ref, a_out), (b_ref, b_out), (c_ref, c_out))
    reads = [
        pltpu.make_async_copy(source, held.at[i], arrived.at[i])
        for i, (source, _) in enumerate(pairs)
    ]
    writes = [
        pltpu.make_async_copy(held.at[i], target, done.at[i])
        for i, (_, target) in enumerate(pairs)
    ]
    for read in reads:
        read.start()
    for read, write in zip(reads, writes):
        read.wait()
        write.start()
    for write in writes:
        write.wait()


def fused_on_device(shards, uly, q, k, v, o, g, random_blocks):
    tok, width = q.shape
    length = tok * uly
    per = length // BLOCK
    dma = pltpu.SemaphoreType.DMA
    hbm = pl.BlockSpec(memory_space=pltpu.HBM)
    results = pl.pallas_call(
        functools.partial(fused_kernel, shards, uly),
        out_shape=[jax.ShapeDtypeStruct((tok, width), jnp.bfloat16)] * 3,
        in_specs=[hbm] * 6,
        out_specs=[hbm] * 3,
        scratch_shapes=[
            pltpu.SMEM(random_blocks.shape[::-1], jnp.int32),
            pltpu.VMEM((2, tok, width), jnp.bfloat16),
            pltpu.VMEM((4, shards, length, HD), jnp.bfloat16),
            pltpu.VMEM((uly, 1, BLOCK), jnp.float32),
            pltpu.VMEM((uly, 1, BLOCK), jnp.float32),
            pltpu.VMEM((shards, shards * per, length), jnp.float32),
            pltpu.VMEM((shards, 2, length), jnp.float32),
            pltpu.VMEM((shards, length, length), jnp.float32),
            pltpu.VMEM((length, length), jnp.bfloat16),
            pltpu.VMEM((length, length), jnp.bfloat16),
            pltpu.VMEM((3, length, HD), jnp.float32),
            pltpu.VMEM((3, length, HD), jnp.bfloat16),
            dma((4, uly)),
            dma((4, uly)),
            dma((4,)),
            dma((uly,)),
            dma((uly,)),
            dma((4, per, shards)),
            dma((4, per, shards)),
            dma((shards,)),
            dma((shards,)),
            dma((3, uly)),
            dma((3, uly)),
            dma((3,)),
            dma((3,)),
        ],
        compiler_params=pltpu.CompilerParams(
            collective_id=0, has_side_effects=True, vmem_limit_bytes=67043328
        ),
    )(random_blocks.T, q, k, v, o, g)
    return pl.pallas_call(
        write_out,
        out_shape=[jax.ShapeDtypeStruct((tok, width), jnp.bfloat16)] * 3,
        in_specs=[hbm] * 3,
        out_specs=[hbm] * 3,
        scratch_shapes=[pltpu.VMEM((3, tok, width), jnp.bfloat16), dma((3,)), dma((3,))],
        compiler_params=pltpu.CompilerParams(vmem_limit_bytes=67043328),
    )(*results)


def wide_or_fused(shards, uly, *operands):
    tok, width = operands[0].shape
    length = tok * uly
    fits = shards * length * length * 4 <= 16 * 1024 * 1024
    if fits and width == uly * HD and BLOCK % tok == 0 and length % BLOCK == 0:
        return tuple(fused_on_device(shards, uly, *operands))
    return on_device(*operands)


def solution(mesh):
    return jax.shard_map(
        functools.partial(wide_or_fused, mesh.shape["blk"], mesh.shape["uly"]),
        mesh=mesh,
        in_specs=(
            P(("blk", "uly"), None),
            P(("blk", "uly"), None),
            P(("blk", "uly"), None),
            P(("blk", "uly"), None),
            P(("blk", "uly"), None),
            P(),
        ),
        out_specs=(P(("blk", "uly"), None), P(("blk", "uly"), None), P(("blk", "uly"), None)),
        check_vma=False,
    )
```
